256 devices in a mesh: expert: 32 (over y, z), ctx: 8 (over x, core).
Axes of the slice: x: 4, y: 4, z: 8, core: 2. Of those that a mesh axis runs over, the one named last changes fastest.
Arguments:
- tokens: bfloat16 [4096, 4096], P('expert', 'ctx'), may hold values from -6 to 6
- grad_out: bfloat16 [4096, 4096], P('expert', 'ctx'), may hold values from -1.5 to 1.5
- expert_ids: int32 [4096, 8], P('expert'), may hold values from 0 to 63, all different within a row; in each aligned block of 128 rows (0 to 127, 128 to 255, ...) at most 18 rows name the same one
- gate_probs: float32 [4096, 8], P('expert'), may hold values from 0.05 to 1
- gate_weight: bfloat16 [64, 1536, 4096], P('expert', 'ctx'), may hold values from -0.09375 to 0.09375
- up_weight: bfloat16 [64, 1536, 4096], P('expert', 'ctx'), may hold values from -0.09375 to 0.09375
- down_weight: bfloat16 [64, 1536, 4096], P('expert', 'ctx'), may hold values from -0.15625 to 0.15625
Outputs:
- grad_tokens: bfloat16 [4096, 4096], P('expert', 'ctx')
- grad_gates: bfloat16 [4096, 8], P('expert')
The draws below stay inside these ranges and needn't reach their ends.
Inputs may be any that keep to these rules, and one draw needn't show every extreme that they name: `expert_ids`: each row names 8 different experts. Within the 128 rows of one index of expert (aligned blocks), no expert is named more than 18 times, and in every draw some expert is named exactly 18 times in some block.
All inputs are finite; a program needn't handle non-finite values.
Results may differ from the reference program's by a relative error of at most 0.014.
Values may be sent and summed in bfloat16 or wider, within the bound.
A program may use at most 128 MiB of HBM per device.

```python
import math
import jax
import jax.numpy as jnp
import numpy as np
from jax import lax

D = 4096
FF = 1536
TOP = 8
TOK_DEV = 128
EXPERTS = 64
TOKENS = 4096
CAP = 18
N_EXPERT = 32
N_CTX = 8


def block_scale(key, extent, split, smallest, high):
    loudness = 1.0
    for position, shards_of in split:
        draws = jax.random.uniform(jax.random.fold_in(jax.random.fold_in(key, 6), position), (shards_of,), jnp.float32, smallest / len(split), high / len(split))
        loudness = loudness * jnp.repeat(jnp.exp(draws), extent[position] // shards_of).reshape((-1,) + (1,) * (len(extent) - 1 - position))
    return loudness


def shared_out(key, own, number, rows, number_of, top, most, skew):
    sequence = jax.random.permutation(key, number_of)
    packed, usual = portions_of(number_of, rows * top, most, skew, True), portions_of(number_of, rows * top, most, skew, False)
    places = jnp.arange(number_of)

    def named(sizes, turn):
        used = int((sizes > 0).sum())
        fixed = max(1, used // 4)
        moved = fixed + (places - fixed + turn * (used - fixed)) % max(1, number_of - fixed)
        return jnp.zeros((number_of,), jnp.int32).at[sequence[jnp.where(places < fixed, places, moved)]].set(jnp.asarray(sizes, jnp.int32))

    sizes = jnp.where(number % 4 == 0, named(packed, number // 4), named(usual, number - number // 4 - 1))
    mixed = jax.random.permutation(jax.random.fold_in(own, 3), number_of)
    source_of, taker = mixed[0:number_of // 2 * 2:2], mixed[1:number_of // 2 * 2:2]
    margin = jnp.minimum(sizes[source_of] - 1, most - sizes[taker]) // 2
    margin = jnp.where((source_of == sequence[0]) | (taker == sequence[0]) | (sizes[taker] == 0), 0, jnp.maximum(margin, 0))
    moved = jax.random.randint(jax.random.fold_in(own, 4), (number_of // 2,), 0, 1 << 20) % (margin + 1)
    sizes = sizes.at[source_of].add(-moved).at[taker].add(moved)
    items = jnp.searchsorted(jnp.cumsum(sizes), jnp.arange(rows * top), side="right").astype(jnp.int32)
    grid = items.reshape(top, rows).T
    grid = grid[jax.random.permutation(jax.random.fold_in(own, 1), rows)]
    turn = jax.random.randint(jax.random.fold_in(own, 2), (rows, 1), 0, top)
    return jnp.take_along_axis(grid, (jnp.arange(top)[None, :] + turn) % top, axis=1)


def portions_of(count, total, reach, slope, full):
    loads = [(1 << 20) // math.isqrt(standing ** slope) + 1 for standing in range(1, count + 1)]
    largest = reach if full else min(reach, max(-(-total // count), total * loads[0] // sum(loads)))
    least = 1 if total - largest >= count - 1 else 0
    given, surplus = [largest] + [least] * (count - 1), total - largest - least * (count - 1)
    while surplus > 0:
        movable = [i for i in range(1, count) if given[i] < largest] or [i for i in range(1, count) if given[i] < reach]
        pool, remaining = sum([loads[i] for i in movable]), surplus
        for i in movable:
            addition = min(reach - given[i], max(1, remaining * loads[i] // pool), surplus)
            given[i] = given[i] + addition
            surplus = surplus - addition
    return np.array(given)


def centred(rng, extent, deviation, reach, pieces=(), held_as=jnp.bfloat16):
    result = deviation * jax.random.normal(rng, extent, jnp.float32)
    if pieces:
        result = result * block_scale(rng, extent, pieces, -0.22, 0.18)
    return jnp.clip(result, -reach, reach).astype(held_as)


def setup_inputs(seed: int = 0) -> dict:
    splits = jax.random.split(jax.random.key(seed), 8)
    tokens = centred(splits[0], (TOKENS, D), 1.0, 6.0, ((0, 32), (1, 8)))
    grad_out = centred(splits[1], (TOKENS, D), 0.25, 1.5, ((0, 32), (1, 8)))
    expert_ids_keys = jax.random.split(jax.random.fold_in(splits[2], 1), TOKENS // TOK_DEV)
    expert_ids_turns = jax.random.permutation(jax.random.fold_in(splits[2], 3), TOKENS // TOK_DEV)
    expert_ids = jax.vmap(lambda own, number: shared_out(jax.random.fold_in(splits[2], 2), own, number, TOK_DEV, EXPERTS, TOP, CAP, 0))(expert_ids_keys, expert_ids_turns).reshape((TOKENS, TOP))
    gate_probs = jnp.clip(jnp.exp(math.log(1.0) - 2.9957323 * jax.random.uniform(splits[3], (TOKENS, TOP), jnp.float32) ** block_scale(splits[3], (TOKENS, TOP), ((0, 32),), -0.2, 0.2)), 0.05, 1.0)
    gate_weight = centred(splits[4], (EXPERTS, FF, D), D ** -0.5, 0.09375, ((0, 32), (1, 8)))
    up_weight = centred(splits[5], (EXPERTS, FF, D), D ** -0.5, 0.09375, ((0, 32), (1, 8)))
    down_weight = centred(splits[6], (EXPERTS, FF, D), FF ** -0.5, 0.15625, ((0, 32), (1, 8)))
    return {"tokens": tokens, "grad_out": grad_out, "expert_ids": expert_ids, "gate_probs": gate_probs, "gate_weight": gate_weight, "up_weight": up_weight, "down_weight": down_weight}


def reference(tokens, grad_out, expert_ids, gate_probs, gate_weight, up_weight, down_weight):
    per_block = TOK_DEV * TOP
    row_count = N_EXPERT * CAP
    ff_block = FF // N_CTX
    blocks = expert_ids.reshape(N_EXPERT, per_block)
    one_hot = (blocks[:, :, None] == jnp.arange(EXPERTS, dtype=jnp.int32)[None, None, :]).astype(jnp.int32)
    earlier = jnp.cumsum(one_hot, axis=1) - one_hot
    slot_rank = jnp.sum(earlier * one_hot, axis=2).astype(jnp.int32)
    block_ids = jnp.broadcast_to(jnp.arange(N_EXPERT, dtype=jnp.int32)[:, None], (N_EXPERT, per_block))
    token_ids = (block_ids * TOK_DEV + jnp.arange(per_block, dtype=jnp.int32)[None, :] // TOP).astype(jnp.int32)
    columns = (block_ids * CAP + slot_rank).astype(jnp.int32)
    index_table = jnp.zeros((EXPERTS, row_count), jnp.int32).at[blocks, columns].set(token_ids)
    filled_table = jnp.zeros((EXPERTS, row_count), jnp.float32).at[blocks, columns].set(1.0)
    weight_table = jnp.zeros((EXPERTS, row_count), jnp.float32).at[blocks, columns].set(gate_probs.reshape(N_EXPERT, per_block))

    def expert_step(running, inputs_row):
        row_index, filled, gate_rows, gate_mat, up_mat, down_mat = inputs_row
        keep = filled[:, None] > 0.5
        rows_in = jnp.where(keep, tokens[row_index], jnp.zeros((), jnp.bfloat16))
        rows_grad = jnp.where(keep, grad_out[row_index], jnp.zeros((), jnp.bfloat16))
        pre_gate = jnp.dot(rows_in, gate_mat.T, preferred_element_type=jnp.float32)
        pre_up = jnp.dot(rows_in, up_mat.T, preferred_element_type=jnp.float32)
        grad_hidden = jnp.dot(rows_grad, down_mat.T, preferred_element_type=jnp.float32)
        sigmoid_gate = jax.nn.sigmoid(pre_gate)
        activated = pre_gate * sigmoid_gate
        gate_score = jnp.sum(activated * pre_up * grad_hidden, axis=1).astype(jnp.bfloat16)
        grad_pre_gate = (grad_hidden * pre_up * sigmoid_gate * (1.0 + pre_gate * (1.0 - sigmoid_gate))).astype(jnp.bfloat16)
        grad_pre_up = (grad_hidden * activated).astype(jnp.bfloat16)
        gpg = grad_pre_gate.astype(jnp.float32).reshape(row_count, N_CTX, ff_block)
        gpu = grad_pre_up.astype(jnp.float32).reshape(row_count, N_CTX, ff_block)
        gate_blocks = gate_mat.astype(jnp.float32).reshape(N_CTX, ff_block, D)
        up_blocks = up_mat.astype(jnp.float32).reshape(N_CTX, ff_block, D)
        block_terms = jnp.einsum("rcf,cfd->crd", gpg, gate_blocks) + jnp.einsum("rcf,cfd->crd", gpu, up_blocks)
        rounded = lax.optimization_barrier(block_terms.astype(jnp.bfloat16))
        combined = jnp.sum(rounded.astype(jnp.float32), axis=0).astype(jnp.bfloat16)
        added = gate_rows[:, None] * combined.astype(jnp.float32) * filled[:, None]
        return running.at[row_index].add(added), gate_score

    start = jnp.zeros((TOKENS, D), jnp.float32)
    running, scores = lax.scan(expert_step, start, (index_table, filled_table, weight_table, gate_weight, up_weight, down_weight))
    grad_gates = scores[blocks, columns].reshape(TOKENS, TOP)
    return running.astype(jnp.bfloat16), grad_gates
```

```python
import jax
import jax.numpy as jnp
from jax import lax
from jax.experimental import pallas as pl
from jax.experimental.pallas import tpu as pltpu
from jax.sharding import PartitionSpec as P

MESH = pl.DeviceIdType.MESH
NY, NZ, NX = 4, 8, 4
CAP, TOK, TOP = 18, 128, 8
R = NZ * CAP
FS, FFL, NF = 512, 192, 8
D = FS * NF
Q = NY * 2
BF, F32 = jnp.bfloat16, jnp.float32


def rc(src, dst, ss, rs, dev):
    return pltpu.make_async_remote_copy(
        src_ref=src, dst_ref=dst, send_sem=ss, recv_sem=rs, device_id=dev, device_id_type=MESH
    )


def kernel(
    tok, grad, meta, wg, wu, wd, out, gg,
    XB, MB, KEY, WT, PLB, GB, RB, WV, PB, PX, RA, RM, FB, YB, T, ZS, ZR,
    SC, SCR, SCT, YSC, SE, ZSC,
    ls, ws, zs, zv, ms, mv, ys, yv, xs, xv, ps, pv, pxs, pxv, as_, av, rs, rv, rys, ryv, zrs, zrv,
    scs, scv, sys_, syv, szs, szv,
):
    me_e, me_c = lax.axis_index("expert"), lax.axis_index("ctx")
    y, z = me_e // NZ, me_e % NZ
    x, c = me_c // 2, me_c % 2

    def xdev(dx):
        return {"ctx": ((x + dx) % NX) * 2 + c}

    partner = {"ctx": x * 2 + 1 - c}

    def ydev(dy):
        return {"expert": ((y + dy) % NY) * NZ + z}

    def zdev(dz):
        return {"expert": y * NZ + (z + dz) % NZ}

    def cdev(k):
        return {"ctx": (me_c + k) % NF}

    loads = [
        pltpu.make_async_copy(tok, XB.at[0, 0], ls.at[0]),
        pltpu.make_async_copy(grad, XB.at[0, 1], ls.at[1]),
        pltpu.make_async_copy(meta, MB.at[0], ls.at[2]),
    ]
    for cp in loads:
        cp.start()

    barrier = pltpu.get_barrier_semaphore()
    peers = [cdev(k) for k in range(1, NF)] + [ydev(k) for k in range(1, NY)]
    peers += [zdev(k) for k in range(1, NZ)]
    for peer in peers:
        pl.semaphore_signal(barrier, inc=1, device_id=peer, device_id_type=MESH)
    pl.semaphore_wait(barrier, len(peers))
    for cp in loads:
        cp.wait()

    def zx(way, s):
        if way == 0:
            si, di, dev, part = (NZ - (s - 1)) % NZ, NZ - s, zdev(1), 0
        else:
            si, di, dev, part = s - 1, s, zdev(NZ - 1), 1
        if s < NZ // 2:
            return rc(XB.at[si], XB.at[di], zs.at[way, s - 1], zv.at[way, s - 1], dev)
        return rc(XB.at[si, part], XB.at[di, part], zs.at[way, s - 1], zv.at[way, s - 1], dev)

    def zm(way, s):
        if way == 0:
            si, di, dev = (NZ - (s - 1)) % NZ, NZ - s, zdev(1)
        else:
            si, di, dev = s - 1, s, zdev(NZ - 1)
        return rc(MB.at[si], MB.at[di], ms.at[way, s - 1], mv.at[way, s - 1], dev)

    lane = lax.broadcasted_iota(jnp.int32, (TOK, TOK), 1)
    sub = lax.broadcasted_iota(jnp.int32, (TOK, TOK), 0)
    before = (sub < lane).astype(BF)
    erow = lax.broadcasted_iota(jnp.int32, (8, TOK), 0)
    dyrow = erow // 2
    expert = (2 * (((y + dyrow) % NY) * NZ + z) + (erow - 2 * dyrow)).astype(F32)

    def key(d):
        member = jnp.zeros((8, TOK), F32)
        weight = jnp.zeros((8, TOK), F32)
        for k in range(TOP):
            hit = jnp.broadcast_to(MB[d, k : k + 1, :], (8, TOK)) == expert
            member = member + jnp.where(hit, 1.0, 0.0)
            prob = jnp.broadcast_to(MB[d, TOP + k : TOP + k + 1, :], (8, TOK))
            weight = weight + jnp.where(hit, prob, 0.0)
        rank = jnp.dot(member.astype(BF), before, preferred_element_type=F32)
        slot = jnp.where(member > 0.5, rank + float(d * CAP), -1.0)
        for e in range(8):
            KEY[e, :, d * TOK : (d + 1) * TOK] = slot[e : e + 1]
            WT[e, :, d * TOK : (d + 1) * TOK] = weight[e : e + 1]

    half = NZ // 2
    for way in range(2):
        zm(way, 1).start()
        zx(way, 1).start()

    def wload(j, f, m):
        xo = (0, NX - 1, 1, 2)[f % 4]
        ctx = ((x + xo) % NX) * 2 + (c if f < 4 else 1 - c)
        src = (wg, wu, wd)[m].at[j, :, pl.ds(pl.multiple_of(ctx * FS, FS), FS)]
        dst = WV.at[j, pl.ds(m * FFL, FFL), pl.ds(f * FS, FS)]
        return pltpu.make_async_copy(src, dst, ws.at[j, f, m])

    wloads = [wload(j, f, m) for j in range(2) for f in range(NF) for m in range(3)]
    for cp in wloads:
        cp.start()

    key(0)
    for s in range(1, half + 1):
        for way in range(2):
            if s < half or way == 0:
                zm(way, s).wait_recv()
                if s + 1 < half or (s + 1 == half and way == 0):
                    zm(way, s + 1).start()
            zx(way, s).wait_recv()
            if s < half:
                zx(way, s + 1).start()
        key(NZ - s)
        if s < half:
            key(s)

    rowid = lax.broadcasted_iota(jnp.int32, (R, NZ * TOK), 0).astype(F32)

    def place(e):
        hit = jnp.broadcast_to(KEY[e], (R, NZ * TOK)) == rowid
        PLB[e] = jnp.where(hit, 1.0, 0.0).astype(BF)

    def gather(e, a):
        slab = XB[:, a].reshape(NZ * TOK, FS)
        return jnp.dot(PLB[e], slab, preferred_element_type=F32).astype(BF)

    def own(q):
        return RB.at[q, :, :, pl.ds(0, FS)]

    def fsl(q, f):
        return RB.at[q, :, :, pl.ds(f * FS, FS)]

    def xr(q):
        return rc(own(q), fsl(q, 1), xs.at[q, 0], xv.at[q, 0], xdev(1))

    def xl(q):
        return rc(own(q), fsl(q, 2), xs.at[q, 1], xv.at[q, 1], xdev(NX - 1))

    def xt(q):
        return rc(
            RB.at[q, 0, :, pl.ds(FS, FS)], RB.at[q, 0, :, pl.ds(3 * FS, FS)],
            xs.at[q, 2], xv.at[q, 2], xdev(1),
        )

    def xg(q):
        return rc(
            RB.at[q, 1, :, pl.ds(2 * FS, FS)], RB.at[q, 1, :, pl.ds(3 * FS, FS)],
            xs.at[q, 3], xv.at[q, 3], xdev(NX - 1),
        )

    def pp(q, f):
        return rc(fsl(q, f), fsl(q, 4 + f), ps.at[q, f], pv.at[q, f], partner)

    def yc(q):
        return rc(GB.at[q - 2], own(q), ys.at[q - 2], yv.at[q - 2], ydev(NY - q // 2))

    def send_own(q):
        xr(q).start()
        xl(q).start()
        pp(q, 0).start()

    @pl.loop(0, 2)
    def _(q):
        place(q)
        for a in range(2):
            RB[q, a, :, 0:FS] = gather(q, a)
        send_own(q)

    @pl.loop(2, Q)
    def _(q):
        e = ((NY - q // 2) % NY) * 2 + q % 2
        place(e)
        for a in range(2):
            GB[q - 2, a] = gather(e, a)
        yc(q).start()

    for cp in wloads:
        cp.wait()
    for d in range(NZ):
        T[d] = jnp.zeros((TOK, FS), F32)

    nt = (((1,), (1,)), ((), ()))
    tn = (((0,), (0,)), ((), ()))

    def px(q):
        return rc(PB.at[q, pl.ds(4, 4)], PX.at[q], pxs.at[q], pxv.at[q], partner)

    def ra(q, w):
        return rc(
            PB.at[q, 3, :, pl.ds(w * (FS // 2), FS // 2)], RA.at[q, w],
            as_.at[q, w], av.at[q, w], xdev(1 if w == 0 else NX - 1),
        )

    def rm(q, w):
        return rc(
            PB.at[q, 2 - w], RM.at[q, w], rs.at[q, w], rv.at[q, w], xdev(1 if w == 0 else NX - 1)
        )

    def ry(q):
        return rc(FB.at[q - 2], YB.at[q], rys.at[q - 2], ryv.at[q - 2], ydev(q // 2))

    def step_a(q):
        yc(q).wait_recv()
        send_own(q)

    def step_b(q):
        xr(q).wait_recv()
        xt(q).start()
        pp(q, 1).start()
        xl(q).wait_recv()
        xg(q).start()
        pp(q, 2).start()

    def step_c(q):
        xt(q).wait_recv()
        xg(q).wait_recv()
        pp(q, 3).start()

    def step_d(q):
        j = q % 2
        for f in range(4):
            pp(q, f).wait_recv()
        pre_gate = lax.dot_general(RB[q, 0], WV[j, 0:FFL, :], nt, preferred_element_type=F32)
        pre_up = lax.dot_general(
            RB[q, 0], WV[j, FFL : 2 * FFL, :], nt, preferred_element_type=F32
        )
        hidden = lax.dot_general(
            RB[q, 1], WV[j, 2 * FFL : 3 * FFL, :], nt, preferred_element_type=F32
        )
        sg = jax.nn.sigmoid(pre_gate)
        act = pre_gate * sg
        prod = act * pre_up * hidden
        hi = prod.astype(BF)
        lo = (prod - hi.astype(F32)).astype(BF)
        ones = jnp.ones((8, FFL), BF)
        score = lax.dot_general(ones, hi, nt, preferred_element_type=F32)
        score = score + lax.dot_general(ones, lo, nt, preferred_element_type=F32)
        SC[q, :, 0:R] = score[0:1]
        gpg = (hidden * pre_up * sg * (1.0 + pre_gate * (1.0 - sg))).astype(BF)
        gpu = (hidden * act).astype(BF)
        for f in (4, 5, 6, 7, 3, 2, 1, 0):
            part = jnp.dot(gpg, WV[j, 0:FFL, f * FS : (f + 1) * FS], preferred_element_type=F32)
            part = part + jnp.dot(
                gpu, WV[j, FFL : 2 * FFL, f * FS : (f + 1) * FS], preferred_element_type=F32
            )
            PB[q, f] = part.astype(BF)
            if f == 7:
                px(q).start()

    def step_e(q):
        px(q).wait_recv()
        for f in (3, 2, 1, 0):
            PB[q, f] = (PB[q, f].astype(F32) + PX[q, f].astype(F32)).astype(BF)
            if f == 3:
                ra(q, 0).start()
                ra(q, 1).start()

    def step_f(q):
        for w in range(2):
            ra(q, w).wait_recv()
            lo, hi = w * (FS // 2), (w + 1) * (FS // 2)
            PB[q, 2 - w, :, lo:hi] = (
                PB[q, 2 - w, :, lo:hi].astype(F32) + RA[q, w].astype(F32)
            ).astype(BF)
            rm(q, w).start()

    def step_g(q):
        rm(q, 0).wait_recv()
        rm(q, 1).wait_recv()
        total = PB[q, 0].astype(F32) + RM[q, 0].astype(F32) + RM[q, 1].astype(F32)

        @pl.when(q < 2)
        def _():
            YB[q] = total.astype(BF)

        @pl.when(q >= 2)
        def _():
            FB[q - 2] = total.astype(BF)
            ry(q).start()

    def step_h(q):
        @pl.when(q >= 2)
        def _():
            ry(q).wait_recv()

        e = ((NY - q // 2) % NY) * 2 + q % 2
        for d in range(NZ):
            pick = PLB[e, :, d * TOK : (d + 1) * TOK].astype(F32)
            pick = pick * jnp.broadcast_to(WT[e, :, d * TOK : (d + 1) * TOK], (R, TOK))
            T[d] += lax.dot_general(pick.astype(BF), YB[q], tn, preferred_element_type=F32)

    def scx(k):
        return rc(SC, SCR.at[me_c], scs.at[k - 1], scv.at[k - 1], cdev(k))

    def scy(k):
        return rc(SCT, YSC.at[k - 1], sys_.at[k - 1], syv.at[k - 1], ydev(NY - k))

    def scz(k):
        return rc(SE.at[k], ZSC.at[NZ - k], szs.at[k - 1], szv.at[k - 1], zdev(k))

    @pl.loop(0, Q + 3)
    def _(i):
        pl.when(i < Q - 2)(lambda: step_a(i + 2))
        pl.when(i < Q)(lambda: step_b(i))
        pl.when((i >= 1) & (i < Q + 1))(lambda: step_e(i - 1))

        @pl.when(i < Q)
        def _():
            step_c(i)
            step_d(i)

        @pl.when(i == Q)
        def _():
            for k in range(1, NF):
                scx(k).start()

        pl.when((i >= 1) & (i < Q + 1))(lambda: step_f(i - 1))
        pl.when((i >= 2) & (i < Q + 2))(lambda: step_g(i - 2))
        pl.when((i >= 3) & (i < Q + 3))(lambda: step_h(i - 3))

    hf = FS // 2

    def zt(way, s):
        dev = zdev(1 if way == 0 else NZ - 1)
        if s == 1:
            lanes = pl.ds(way * hf, hf)
            src, dst = ZS.at[way, 0, :, lanes], ZR.at[way, 0, :, lanes]
        else:
            src, dst = ZS.at[way, s - 1], ZR.at[way, s - 1]
        return rc(src, dst, zrs.at[way, s - 1], zrv.at[way, s - 1], dev)

    for way in range(2):
        lanes = slice(way * hf, (way + 1) * hf)
        ZS[way, 0, :, lanes] = T[half, :, lanes].astype(BF)
        zt(way, 1).start()

    SCR[me_c] = SC[...]
    for k in range(1, NF):
        scx(k).wait_recv()
    total = SCR[0]
    for k in range(1, NF):
        total = total + SCR[k]
    SCT[...] = total
    for k in range(1, NY):
        scy(k).start()

    def ring(s):
        for way in range(2):
            zt(way, s - 1).wait_recv()
            d = half - (s - 1) if way == 0 else half + (s - 1)
            if s == 2:
                lanes = slice(way * hf, (way + 1) * hf)
                other = slice((1 - way) * hf, (2 - way) * hf)
                ZS[way, 1, :, lanes] = (
                    T[d, :, lanes] + ZR[way, 0, :, lanes].astype(F32)
                ).astype(BF)
                ZS[way, 1, :, other] = T[d, :, other].astype(BF)
            else:
                ZS[way, s - 1] = (T[d] + ZR[way, s - 2].astype(F32)).astype(BF)
            zt(way, s).start()

    ring(2)
    for dy in range(NY):
        if dy:
            scy(dy).wait_recv()
        for j in range(2):
            e = dy * 2 + j
            row = ((NY - dy) % NY) * 2 + j
            table = SCT[row, :, 0:R] if dy == 0 else YSC[dy - 1, row, :, 0:R]
            table = jnp.broadcast_to(table, (8, R))
            hi = table.astype(BF)
            lo = (table - hi.astype(F32)).astype(BF)
            spread = jnp.dot(hi, PLB[e], preferred_element_type=F32)
            spread = spread + jnp.dot(lo, PLB[e], preferred_element_type=F32)
            for d in range(NZ):
                SE[d, e : e + 1, :] = spread[0:1, d * TOK : (d + 1) * TOK]
    for k in range(1, NZ):
        scz(k).start()
    for s in range(3, half + 1):
        ring(s)

    gates = jnp.zeros((TOP, TOK), F32)
    ids = MB[0, 0:TOP, :]
    for d in range(NZ):
        if d:
            scz(NZ - d).wait_recv()
        piece = SE[0] if d == 0 else ZSC[d]
        for i in range(8):
            who = (2 * (((y + i // 2) % NY) * NZ + (z + d) % NZ) + i % 2).astype(F32)
            gates = gates + jnp.where(
                ids == who, jnp.broadcast_to(piece[i : i + 1, :], (TOP, TOK)), 0.0
            )
    gg[...] = gates

    for way in range(2):
        zt(way, half).wait_recv()
    out[...] = (
        T[0] + ZR[0, half - 1].astype(F32) + ZR[1, half - 1].astype(F32)
    ).astype(BF)

    for s in range(1, half + 1):
        for way in range(2):
            if s < half or way == 0:
                zm(way, s).wait_send()
            zx(way, s).wait_send()
            zt(way, s).wait_send()

    @pl.loop(0, Q)
    def _(q):
        for cp in (xr(q), xl(q), xt(q), xg(q), px(q), ra(q, 0), ra(q, 1), rm(q, 0), rm(q, 1)):
            cp.wait_send()
        for f in range(4):
            pp(q, f).wait_send()

    @pl.loop(2, Q)
    def _(q):
        yc(q).wait_send()
        ry(q).wait_send()

    for k in range(1, NF):
        scx(k).wait_send()
    for k in range(1, NY):
        scy(k).wait_send()
    for k in range(1, NZ):
        scz(k).wait_send()


def body(tokens, grad_out, expert_ids, gate_probs, gate_weight, up_weight, down_weight):
    meta = jnp.concatenate([expert_ids.astype(F32), gate_probs], axis=1).T
    V, S = pltpu.VMEM, pltpu.SemaphoreType.DMA
    scratch = [
        V((NZ, 2, TOK, FS), BF), V((NZ, 2 * TOP, TOK), F32),
        V((8, 1, NZ * TOK), F32), V((8, 1, NZ * TOK), F32), V((8, R, NZ * TOK), BF),
        V((Q - 2, 2, R, FS), BF), V((Q, 2, R, D), BF), V((2, 3 * FFL, D), BF),
        V((Q, NF, R, FS), BF), V((Q, 4, R, FS), BF), V((Q, 2, R, FS // 2), BF),
        V((Q, 2, R, FS), BF), V((Q - 2, R, FS), BF), V((Q, R, FS), BF),
        V((NZ, TOK, FS), F32), V((2, NZ // 2, TOK, FS), BF), V((2, NZ // 2, TOK, FS), BF),
        V((Q, 1, 256), F32), V((NF, Q, 1, 256), F32), V((Q, 1, 256), F32),
        V((NY - 1, Q, 1, 256), F32),
        V((NZ, 8, TOK), F32), V((NZ, 8, TOK), F32),
        S((3,)), S((2, NF, 3)),
        S((2, 4)), S((2, 4)), S((2, 4)), S((2, 4)), S((Q - 2,)), S((Q - 2,)),
        S((Q, 4)), S((Q, 4)), S((Q, 4)), S((Q, 4)), S((Q,)), S((Q,)),
        S((Q, 2)), S((Q, 2)), S((Q, 2)), S((Q, 2)), S((Q - 2,)), S((Q - 2,)), S((2, 4)), S((2, 4)),
        S((NF - 1,)), S((NF - 1,)), S((NY - 1,)), S((NY - 1,)), S((NZ - 1,)), S((NZ - 1,)),
    ]
    anyspec = pl.BlockSpec(memory_space=pl.ANY)
    vmem = pl.BlockSpec(memory_space=pltpu.VMEM)
    out, gates = pl.pallas_call(
        kernel,
        out_shape=(
            jax.ShapeDtypeStruct((TOK, FS), BF),
            jax.ShapeDtypeStruct((TOP, TOK), F32),
        ),
        in_specs=[anyspec] * 6,
        out_specs=(vmem, vmem),
        scratch_shapes=scratch,
        compiler_params=pltpu.CompilerParams(
            collective_id=0, has_side_effects=True, vmem_limit_bytes=60 * 1024 * 1024
        ),
        name="expert_grad",
    )(tokens, grad_out, meta, gate_weight, up_weight, down_weight)
    return out, gates.T.astype(BF)


def solution(mesh):
    in_specs = (
        P("expert", "ctx"),
        P("expert", "ctx"),
        P("expert", None),
        P("expert", None),
        P("expert", "ctx", None),
        P("expert", "ctx", None),
        P("expert", "ctx", None),
    )
    out_specs = (P("expert", "ctx"), P("expert", None))
    return jax.shard_map(body, mesh=mesh, in_specs=in_specs, out_specs=out_specs, check_vma=False)
```

```python
import jax
import jax.numpy as jnp
from jax import lax
from jax.experimental import pallas as pl
from jax.experimental.pallas import tpu as pltpu
from jax.sharding import PartitionSpec as P

MESH = pl.DeviceIdType.MESH
NY, NZ, NX = 4, 8, 4
CAP, TOK, TOP = 18, 128, 8
R = NZ * CAP
FS, FFL, NF = 512, 192, 8
D = FS * NF
Q = NY * 2
BF, F32 = jnp.bfloat16, jnp.float32


def rc(src, dst, ss, rs, dev):
    return pltpu.make_async_remote_copy(
        src_ref=src, dst_ref=dst, send_sem=ss, recv_sem=rs, device_id=dev, device_id_type=MESH
    )


def kernel(
    tok, grad, ids_in, probs_in, wg, wu, wd, out, gg,
    XB, MB, KEY, WT, PLB, GB, RB, WV, PB, PX, RA, RM, FB, YB, T, ZS, ZR,
    SC, SCR, SCT, YSC, SE, ZSC,
    ls, ws, zs, zv, ms, mv, ys, yv, xs, xv, ps, pv, pxs, pxv, as_, av, rs, rv, rys, ryv, zrs, zrv,
    scs, scv, sys_, syv, szs, szv,
):
    me_e, me_c = lax.axis_index("expert"), lax.axis_index("ctx")
    y, z = me_e // NZ, me_e % NZ
    x, c = me_c // 2, me_c % 2

    def xdev(dx):
        return {"ctx": ((x + dx) % NX) * 2 + c}

    partner = {"ctx": x * 2 + 1 - c}

    def ydev(dy):
        return {"expert": ((y + dy) % NY) * NZ + z}

    def zdev(dz):
        return {"expert": y * NZ + (z + dz) % NZ}

    def cdev(k):
        return {"ctx": (me_c + k) % NF}

    loads = [
        pltpu.make_async_copy(tok, XB.at[0, 0], ls.at[0]),
        pltpu.make_async_copy(grad, XB.at[0, 1], ls.at[1]),
    ]
    for cp in loads:
        cp.start()

    MB[0, 0:TOP, :] = ids_in[...].astype(F32)
    MB[0, TOP : 2 * TOP, :] = probs_in[...]

    barrier = pltpu.get_barrier_semaphore()
    peers = [cdev(k) for k in range(1, NF)] + [ydev(k) for k in range(1, NY)]
    peers += [zdev(k) for k in range(1, NZ)]
    for peer in peers:
        pl.semaphore_signal(barrier, inc=1, device_id=peer, device_id_type=MESH)
    pl.semaphore_wait(barrier, len(peers))
    for cp in loads:
        cp.wait()

    def zx(way, s, a):
        if way == 0:
            si, di, dev = (NZ - (s - 1)) % NZ, NZ - s, zdev(1)
        else:
            si, di, dev = s - 1, s, zdev(NZ - 1)
        return rc(XB.at[si, a], XB.at[di, a], zs.at[way, s - 1, a], zv.at[way, s - 1, a], dev)

    def zm(way, s):
        if way == 0:
            si, di, dev = (NZ - (s - 1)) % NZ, NZ - s, zdev(1)
        else:
            si, di, dev = s - 1, s, zdev(NZ - 1)
        return rc(MB.at[si], MB.at[di], ms.at[way, s - 1], mv.at[way, s - 1], dev)

    lane = lax.broadcasted_iota(jnp.int32, (TOK, TOK), 1)
    sub = lax.broadcasted_iota(jnp.int32, (TOK, TOK), 0)
    before = (sub < lane).astype(BF)
    erow = lax.broadcasted_iota(jnp.int32, (8, TOK), 0)
    dyrow = erow // 2
    expert = (2 * (((y + dyrow) % NY) * NZ + z) + (erow - 2 * dyrow)).astype(F32)

    def key(d):
        member = jnp.zeros((8, TOK), F32)
        weight = jnp.zeros((8, TOK), F32)
        for k in range(TOP):
            hit = jnp.broadcast_to(MB[d, k : k + 1, :], (8, TOK)) == expert
            member = member + jnp.where(hit, 1.0, 0.0)
            prob = jnp.broadcast_to(MB[d, TOP + k : TOP + k + 1, :], (8, TOK))
            weight = weight + jnp.where(hit, prob, 0.0)
        rank = jnp.dot(member.astype(BF), before, preferred_element_type=F32)
        slot = jnp.where(member > 0.5, rank + float(d * CAP), -1.0)
        for e in range(8):
            KEY[e, :, d * TOK : (d + 1) * TOK] = slot[e : e + 1]
            WT[e, :, d * TOK : (d + 1) * TOK] = weight[e : e + 1]

    half = NZ // 2
    for way in range(2):
        zm(way, 1).start()
    for a in range(2):
        for way in range(2):
            zx(way, 1, a).start()

    def wload(j, f, m):
        xo = (0, NX - 1, 1, 2)[f % 4]
        ctx = ((x + xo) % NX) * 2 + (c if f < 4 else 1 - c)
        src = (wg, wu, wd)[m].at[j, :, pl.ds(pl.multiple_of(ctx * FS, FS), FS)]
        dst = WV.at[j, pl.ds(m * FFL, FFL), pl.ds(f * FS, FS)]
        return pltpu.make_async_copy(src, dst, ws.at[j, f, m])

    wloads = [wload(j, f, m) for j in range(2) for f in range(NF) for m in range(3)]
    for cp in wloads:
        cp.start()

    key(0)
    for s in range(1, half + 1):
        for way in range(2):
            if s < half or way == 0:
                zm(way, s).wait_recv()
                if s + 1 < half or (s + 1 == half and way == 0):
                    zm(way, s + 1).start()
        for a in range(2):
            for way in range(2):
                if s < half or a == way:
                    zx(way, s, a).wait_recv()
                if s + 1 < half or (s + 1 == half and a == way):
                    zx(way, s + 1, a).start()
        key(NZ - s)
        if s < half:
            key(s)

    rowid = lax.broadcasted_iota(jnp.int32, (R, NZ * TOK), 0).astype(F32)

    def place(e):
        hit = jnp.broadcast_to(KEY[e], (R, NZ * TOK)) == rowid
        PLB[e] = jnp.where(hit, 1.0, 0.0).astype(BF)

    def gather(e, a):
        slab = XB[:, a].reshape(NZ * TOK, FS)
        return jnp.dot(PLB[e], slab, preferred_element_type=F32).astype(BF)

    def own(q):
        return RB.at[q, :, :, pl.ds(0, FS)]

    def fsl(q, f):
        return RB.at[q, :, :, pl.ds(f * FS, FS)]

    def xr(q):
        return rc(own(q), fsl(q, 1), xs.at[q, 0], xv.at[q, 0], xdev(1))

    def xl(q):
        return rc(own(q), fsl(q, 2), xs.at[q, 1], xv.at[q, 1], xdev(NX - 1))

    def xt(q):
        return rc(
            RB.at[q, 0, :, pl.ds(FS, FS)], RB.at[q, 0, :, pl.ds(3 * FS, FS)],
            xs.at[q, 2], xv.at[q, 2], xdev(1),
        )

    def xg(q):
        return rc(
            RB.at[q, 1, :, pl.ds(2 * FS, FS)], RB.at[q, 1, :, pl.ds(3 * FS, FS)],
            xs.at[q, 3], xv.at[q, 3], xdev(NX - 1),
        )

    def pp(q, f):
        return rc(fsl(q, f), fsl(q, 4 + f), ps.at[q, f], pv.at[q, f], partner)

    def yc(q):
        return rc(GB.at[q - 2], own(q), ys.at[q - 2], yv.at[q - 2], ydev(NY - q // 2))

    def send_own(q):
        xr(q).start()
        xl(q).start()
        pp(q, 0).start()

    @pl.loop(0, 2)
    def _(q):
        place(q)
        for a in range(2):
            RB[q, a, :, 0:FS] = gather(q, a)
        send_own(q)

    @pl.loop(2, Q)
    def _(q):
        e = ((NY - q // 2) % NY) * 2 + q % 2
        place(e)
        for a in range(2):
            GB[q - 2, a] = gather(e, a)
        yc(q).start()

    for cp in wloads:
        cp.wait()
    for d in range(NZ):
        T[d] = jnp.zeros((TOK, FS), F32)

    nt = (((1,), (1,)), ((), ()))
    tn = (((0,), (0,)), ((), ()))

    def px(q):
        return rc(PB.at[q, pl.ds(4, 4)], PX.at[q], pxs.at[q], pxv.at[q], partner)

    def ra(q, w):
        return rc(
            PB.at[q, 3, :, pl.ds(w * (FS // 2), FS // 2)], RA.at[q, w],
            as_.at[q, w], av.at[q, w], xdev(1 if w == 0 else NX - 1),
        )

    def rm(q, w):
        return rc(
            PB.at[q, 2 - w], RM.at[q, w], rs.at[q, w], rv.at[q, w], xdev(1 if w == 0 else NX - 1)
        )

    def ry(q):
        return rc(FB.at[q - 2], YB.at[q], rys.at[q - 2], ryv.at[q - 2], ydev(q // 2))

    def step_a(q):
        yc(q).wait_recv()
        send_own(q)

    def step_b(q):
        xr(q).wait_recv()
        xt(q).start()
        pp(q, 1).start()
        xl(q).wait_recv()
        xg(q).start()
        pp(q, 2).start()

    def step_c(q):
        xt(q).wait_recv()
        xg(q).wait_recv()
        pp(q, 3).start()

    def step_d(q):
        j = q % 2
        for f in range(4):
            pp(q, f).wait_recv()
        pre_gate = lax.dot_general(RB[q, 0], WV[j, 0:FFL, :], nt, preferred_element_type=F32)
        pre_up = lax.dot_general(
            RB[q, 0], WV[j, FFL : 2 * FFL, :], nt, preferred_element_type=F32
        )
        hidden = lax.dot_general(
            RB[q, 1], WV[j, 2 * FFL : 3 * FFL, :], nt, preferred_element_type=F32
        )
        sg = jax.nn.sigmoid(pre_gate)
        act = pre_gate * sg
        prod = act * pre_up * hidden
        hi = prod.astype(BF)
        lo = (prod - hi.astype(F32)).astype(BF)
        ones = jnp.ones((8, FFL), BF)
        score = lax.dot_general(ones, hi, nt, preferred_element_type=F32)
        score = score + lax.dot_general(ones, lo, nt, preferred_element_type=F32)
        SC[q, :, 0:R] = score[0:1]
        gpg = (hidden * pre_up * sg * (1.0 + pre_gate * (1.0 - sg))).astype(BF)
        gpu = (hidden * act).astype(BF)
        for f in (4, 5, 6, 7, 3, 2, 1, 0):
            part = jnp.dot(gpg, WV[j, 0:FFL, f * FS : (f + 1) * FS], preferred_element_type=F32)
            part = part + jnp.dot(
                gpu, WV[j, FFL : 2 * FFL, f * FS : (f + 1) * FS], preferred_element_type=F32
            )
            PB[q, f] = part.astype(BF)
            if f == 7:
                px(q).start()

    def step_e(q):
        px(q).wait_recv()
        for f in (3, 2, 1, 0):
            PB[q, f] = (PB[q, f].astype(F32) + PX[q, f].astype(F32)).astype(BF)
            if f == 3:
                ra(q, 0).start()
                ra(q, 1).start()

    def step_f(q):
        for w in range(2):
            ra(q, w).wait_recv()
            lo, hi = w * (FS // 2), (w + 1) * (FS // 2)
            PB[q, 2 - w, :, lo:hi] = (
                PB[q, 2 - w, :, lo:hi].astype(F32) + RA[q, w].astype(F32)
            ).astype(BF)
            rm(q, w).start()

    def step_g(q):
        rm(q, 0).wait_recv()
        rm(q, 1).wait_recv()
        total = PB[q, 0].astype(F32) + RM[q, 0].astype(F32) + RM[q, 1].astype(F32)

        @pl.when(q < 2)
        def _():
            YB[q] = total.astype(BF)

        @pl.when(q >= 2)
        def _():
            FB[q - 2] = total.astype(BF)
            ry(q).start()

    def step_h(q):
        @pl.when(q >= 2)
        def _():
            ry(q).wait_recv()

        e = ((NY - q // 2) % NY) * 2 + q % 2
        for d in range(NZ):
            pick = PLB[e, :, d * TOK : (d + 1) * TOK].astype(F32)
            pick = pick * jnp.broadcast_to(WT[e, :, d * TOK : (d + 1) * TOK], (R, TOK))
            T[d] += lax.dot_general(pick.astype(BF), YB[q], tn, preferred_element_type=F32)

    def scx(k):
        return rc(SC, SCR.at[me_c], scs.at[k - 1], scv.at[k - 1], cdev(k))

    def scy(k):
        return rc(SCT, YSC.at[k - 1], sys_.at[k - 1], syv.at[k - 1], ydev(NY - k))

    def scz(k):
        return rc(SE.at[k], ZSC.at[NZ - k], szs.at[k - 1], szv.at[k - 1], zdev(k))

    def during(q, run):
        pl.when((q >= 0) & (q < Q))(lambda: run(q))

    @pl.loop(0, Q + 5)
    def _(t):
        pl.when((t >= 1) & (t < Q - 1))(lambda: step_a(t + 1))
        during(t, step_b)
        during(t - 2, step_e)
        during(t - 1, step_c)
        during(t - 1, step_d)

        @pl.when(t == Q)
        def _():
            for k in range(1, NF):
                scx(k).start()

        during(t - 3, step_f)
        during(t - 4, step_g)
        during(t - 5, step_h)

    hf = FS // 2

    def zt(way, s):
        dev = zdev(1 if way == 0 else NZ - 1)
        if s == 1:
            lanes = pl.ds(way * hf, hf)
            src, dst = ZS.at[way, 0, :, lanes], ZR.at[way, 0, :, lanes]
        else:
            src, dst = ZS.at[way, s - 1], ZR.at[way, s - 1]
        return rc(src, dst, zrs.at[way, s - 1], zrv.at[way, s - 1], dev)

    for way in range(2):
        lanes = slice(way * hf, (way + 1) * hf)
        ZS[way, 0, :, lanes] = T[half, :, lanes].astype(BF)
        zt(way, 1).start()

    SCR[me_c] = SC[...]
    for k in range(1, NF):
        scx(k).wait_recv()
    total = SCR[0]
    for k in range(1, NF):
        total = total + SCR[k]
    SCT[...] = total
    for k in range(1, NY):
        scy(k).start()

    def ring(s):
        for way in range(2):
            zt(way, s - 1).wait_recv()
            d = half - (s - 1) if way == 0 else half + (s - 1)
            if s == 2:
                lanes = slice(way * hf, (way + 1) * hf)
                other = slice((1 - way) * hf, (2 - way) * hf)
                ZS[way, 1, :, lanes] = (
                    T[d, :, lanes] + ZR[way, 0, :, lanes].astype(F32)
                ).astype(BF)
                ZS[way, 1, :, other] = T[d, :, other].astype(BF)
            else:
                ZS[way, s - 1] = (T[d] + ZR[way, s - 2].astype(F32)).astype(BF)
            zt(way, s).start()

    ring(2)
    for dy in range(NY):
        if dy:
            scy(dy).wait_recv()
        for j in range(2):
            e = dy * 2 + j
            row = ((NY - dy) % NY) * 2 + j
            table = SCT[row, :, 0:R] if dy == 0 else YSC[dy - 1, row, :, 0:R]
            table = jnp.broadcast_to(table, (8, R))
            hi = table.astype(BF)
            lo = (table - hi.astype(F32)).astype(BF)
            spread = jnp.dot(hi, PLB[e], preferred_element_type=F32)
            spread = spread + jnp.dot(lo, PLB[e], preferred_element_type=F32)
            for d in range(NZ):
                SE[d, e : e + 1, :] = spread[0:1, d * TOK : (d + 1) * TOK]
    for k in range(1, NZ):
        scz(k).start()
    for s in range(3, half + 1):
        ring(s)

    gates = jnp.zeros((TOP, TOK), F32)
    ids = MB[0, 0:TOP, :]
    for d in range(NZ):
        if d:
            scz(NZ - d).wait_recv()
        piece = SE[0] if d == 0 else ZSC[d]
        for i in range(8):
            who = (2 * (((y + i // 2) % NY) * NZ + (z + d) % NZ) + i % 2).astype(F32)
            gates = gates + jnp.where(
                ids == who, jnp.broadcast_to(piece[i : i + 1, :], (TOP, TOK)), 0.0
            )
    gg[...] = gates.astype(BF)

    for way in range(2):
        zt(way, half).wait_recv()
    out[...] = (
        T[0] + ZR[0, half - 1].astype(F32) + ZR[1, half - 1].astype(F32)
    ).astype(BF)

    for s in range(1, half + 1):
        for way in range(2):
            if s < half or way == 0:
                zm(way, s).wait_send()
            for a in range(2):
                if s < half or a == way:
                    zx(way, s, a).wait_send()
            zt(way, s).wait_send()

    @pl.loop(0, Q)
    def _(q):
        for cp in (xr(q), xl(q), xt(q), xg(q), px(q), ra(q, 0), ra(q, 1), rm(q, 0), rm(q, 1)):
            cp.wait_send()
        for f in range(4):
            pp(q, f).wait_send()

    @pl.loop(2, Q)
    def _(q):
        yc(q).wait_send()
        ry(q).wait_send()

    for k in range(1, NF):
        scx(k).wait_send()
    for k in range(1, NY):
        scy(k).wait_send()
    for k in range(1, NZ):
        scz(k).wait_send()


def body(tokens, grad_out, expert_ids, gate_probs, gate_weight, up_weight, down_weight):
    V, S = pltpu.VMEM, pltpu.SemaphoreType.DMA
    scratch = [
        V((NZ, 2, TOK, FS), BF), V((NZ, 2 * TOP, TOK), F32),
        V((8, 1, NZ * TOK), F32), V((8, 1, NZ * TOK), F32), V((8, R, NZ * TOK), BF),
        V((Q - 2, 2, R, FS), BF), V((Q, 2, R, D), BF), V((2, 3 * FFL, D), BF),
        V((Q, NF, R, FS), BF), V((Q, 4, R, FS), BF), V((Q, 2, R, FS // 2), BF),
        V((Q, 2, R, FS), BF), V((Q - 2, R, FS), BF), V((Q, R, FS), BF),
        V((NZ, TOK, FS), F32), V((2, NZ // 2, TOK, FS), BF), V((2, NZ // 2, TOK, FS), BF),
        V((Q, 1, 256), F32), V((NF, Q, 1, 256), F32), V((Q, 1, 256), F32),
        V((NY - 1, Q, 1, 256), F32),
        V((NZ, 8, TOK), F32), V((NZ, 8, TOK), F32),
        S((2,)), S((2, NF, 3)),
        S((2, 4, 2)), S((2, 4, 2)), S((2, 4)), S((2, 4)), S((Q - 2,)), S((Q - 2,)),
        S((Q, 4)), S((Q, 4)), S((Q, 4)), S((Q, 4)), S((Q,)), S((Q,)),
        S((Q, 2)), S((Q, 2)), S((Q, 2)), S((Q, 2)), S((Q - 2,)), S((Q - 2,)), S((2, 4)), S((2, 4)),
        S((NF - 1,)), S((NF - 1,)), S((NY - 1,)), S((NY - 1,)), S((NZ - 1,)), S((NZ - 1,)),
    ]
    anyspec = pl.BlockSpec(memory_space=pl.ANY)
    vmem = pl.BlockSpec(memory_space=pltpu.VMEM)
    out, gates = pl.pallas_call(
        kernel,
        out_shape=(
            jax.ShapeDtypeStruct((TOK, FS), BF),
            jax.ShapeDtypeStruct((TOP, TOK), BF),
        ),
        in_specs=[anyspec] * 2 + [vmem] * 2 + [anyspec] * 3,
        out_specs=(vmem, vmem),
        scratch_shapes=scratch,
        compiler_params=pltpu.CompilerParams(
            collective_id=0, has_side_effects=True, vmem_limit_bytes=60 * 1024 * 1024
        ),
        name="expert_grad",
    )(tokens, grad_out, expert_ids.T, gate_probs.T, gate_weight, up_weight, down_weight)
    return out, gates.T


def solution(mesh):
    in_specs = (
        P("expert", "ctx"),
        P("expert", "ctx"),
        P("expert", None),
        P("expert", None),
        P("expert", "ctx", None),
        P("expert", "ctx", None),
        P("expert", "ctx", None),
    )
    out_specs = (P("expert", "ctx"), P("expert", None))
    return jax.shard_map(body, mesh=mesh, in_specs=in_specs, out_specs=out_specs, check_vma=False)
```

```python
import jax
import jax.numpy as jnp
from jax import lax
from jax.experimental import pallas as pl
from jax.experimental.pallas import tpu as pltpu
from jax.sharding import PartitionSpec as P

MESH = pl.DeviceIdType.MESH
NY, NZ, NX = 4, 8, 4
CAP, TOK, TOP = 18, 128, 8
R = NZ * CAP
FS, FFL, NF = 512, 192, 8
D = FS * NF
Q = NY * 2
BF, F32 = jnp.bfloat16, jnp.float32


def rc(src, dst, ss, rs, dev):
    return pltpu.make_async_remote_copy(
        src_ref=src, dst_ref=dst, send_sem=ss, recv_sem=rs, device_id=dev, device_id_type=MESH
    )


def kernel(
    tok, grad, ids_in, probs_in, wg, wu, wd, out, gg,
    XB, XA, MB, KEY, WT, PLB, GB, GA, RB, WV, PB, PX, RA, RM, FB, YB, T, ZS, ZR,
    SC, SCR, SCT, YSC, SE, ZSC,
    ls, ws, zs, zv, zas, zav, xas, xav, ms, mv, ys, yv, yas, yav, xs, xv, ps, pv, pxs, pxv, as_, av, rs, rv, rys, ryv, zrs, zrv,
    scs, scv, sys_, syv, szs, szv,
):
    me_e, me_c = lax.axis_index("expert"), lax.axis_index("ctx")
    y, z = me_e // NZ, me_e % NZ
    x, c = me_c // 2, me_c % 2

    def xdev(dx):
        return {"ctx": ((x + dx) % NX) * 2 + c}

    partner = {"ctx": x * 2 + 1 - c}

    def ydev(dy):
        return {"expert": ((y + dy) % NY) * NZ + z}

    def zdev(dz):
        return {"expert": y * NZ + (z + dz) % NZ}

    def cdev(k):
        return {"ctx": (me_c + k) % NF}

    loads = [
        pltpu.make_async_copy(tok, XB.at[0, 0], ls.at[0]),
        pltpu.make_async_copy(grad, XB.at[0, 1], ls.at[1]),
    ]
    for cp in loads:
        cp.start()

    MB[0, 0:TOP, :] = ids_in[...].astype(F32)
    MB[0, TOP : 2 * TOP, :] = probs_in[...]

    barrier = pltpu.get_barrier_semaphore()
    peers = [cdev(k) for k in range(1, NF)] + [ydev(k) for k in range(1, NY)]
    peers += [zdev(k) for k in range(1, NZ)]
    for peer in peers:
        pl.semaphore_signal(barrier, inc=1, device_id=peer, device_id_type=MESH)
    pl.semaphore_wait(barrier, len(peers))
    for cp in loads:
        cp.wait()

    def zx(way, s, a):
        if way == 0:
            si, di, dev = (NZ - (s - 1)) % NZ, NZ - s, zdev(1)
        else:
            si, di, dev = s - 1, s, zdev(NZ - 1)
        return rc(XB.at[si, a], XB.at[di, a], zs.at[way, s - 1, a], zv.at[way, s - 1, a], dev)

    def za(way, s, a):
        if way == 0:
            si, di, dev = (NZ - (s - 1)) % NZ, NZ - s, zdev(1)
        else:
            si, di, dev = s - 1, s, zdev(NZ - 1)
        return rc(XA.at[si, a], XA.at[di, a], zas.at[way, s - 1, a], zav.at[way, s - 1, a], dev)

    def xa(a):
        return rc(XB.at[0, a], XA.at[0, a], xas.at[a], xav.at[a], xdev(2))

    def zm(way, s):
        if way == 0:
            si, di, dev = (NZ - (s - 1)) % NZ, NZ - s, zdev(1)
        else:
            si, di, dev = s - 1, s, zdev(NZ - 1)
        return rc(MB.at[si], MB.at[di], ms.at[way, s - 1], mv.at[way, s - 1], dev)

    lane = lax.broadcasted_iota(jnp.int32, (TOK, TOK), 1)
    sub = lax.broadcasted_iota(jnp.int32, (TOK, TOK), 0)
    before = (sub < lane).astype(BF)
    erow = lax.broadcasted_iota(jnp.int32, (8, TOK), 0)
    dyrow = erow // 2
    expert = (2 * (((y + dyrow) % NY) * NZ + z) + (erow - 2 * dyrow)).astype(F32)

    def key(d):
        member = jnp.zeros((8, TOK), F32)
        weight = jnp.zeros((8, TOK), F32)
        for k in range(TOP):
            hit = jnp.broadcast_to(MB[d, k : k + 1, :], (8, TOK)) == expert
            member = member + jnp.where(hit, 1.0, 0.0)
            prob = jnp.broadcast_to(MB[d, TOP + k : TOP + k + 1, :], (8, TOK))
            weight = weight + jnp.where(hit, prob, 0.0)
        rank = jnp.dot(member.astype(BF), before, preferred_element_type=F32)
        slot = jnp.where(member > 0.5, rank + float(d * CAP), -1.0)
        for e in range(8):
            KEY[e, :, d * TOK : (d + 1) * TOK] = slot[e : e + 1]
            WT[e, :, d * TOK : (d + 1) * TOK] = weight[e : e + 1]

    half = NZ // 2
    for way in range(2):
        zm(way, 1).start()
    for a in range(2):
        for way in range(2):
            zx(way, 1, a).start()
    for a in range(2):
        xa(a).start()

    def wload(j, f, m):
        xo = (0, NX - 1, 1, 2)[f % 4]
        ctx = ((x + xo) % NX) * 2 + (c if f < 4 else 1 - c)
        src = (wg, wu, wd)[m].at[j, :, pl.ds(pl.multiple_of(ctx * FS, FS), FS)]
        dst = WV.at[j, pl.ds(m * FFL, FFL), pl.ds(f * FS, FS)]
        return pltpu.make_async_copy(src, dst, ws.at[j, f, m])

    wloads = [wload(j, f, m) for j in range(2) for f in range(NF) for m in range(3)]
    for cp in wloads:
        cp.start()

    key(0)
    for s in range(1, half + 1):
        for way in range(2):
            if s < half or way == 0:
                zm(way, s).wait_recv()
                if s + 1 < half or (s + 1 == half and way == 0):
                    zm(way, s + 1).start()
        for a in range(2):
            for way in range(2):
                if s < half or a == way:
                    zx(way, s, a).wait_recv()
                if s + 1 < half or (s + 1 == half and a == way):
                    zx(way, s + 1, a).start()
        if s == half - 1:
            for a in range(2):
                xa(a).wait_recv()
                for way in range(2):
                    za(way, 1, a).start()
        key(NZ - s)
        if s < half:
            key(s)

    rowid = lax.broadcasted_iota(jnp.int32, (R, NZ * TOK), 0).astype(F32)

    def place(e):
        hit = jnp.broadcast_to(KEY[e], (R, NZ * TOK)) == rowid
        PLB[e] = jnp.where(hit, 1.0, 0.0).astype(BF)

    def gather(e, a, slabs):
        slab = slabs[:, a].reshape(NZ * TOK, FS)
        return jnp.dot(PLB[e], slab, preferred_element_type=F32).astype(BF)

    def own(q):
        return RB.at[q, :, :, pl.ds(0, FS)]

    def fsl(q, f):
        return RB.at[q, :, :, pl.ds(f * FS, FS)]

    def xr(q):
        return rc(own(q), fsl(q, 1), xs.at[q, 0], xv.at[q, 0], xdev(1))

    def xl(q):
        return rc(own(q), fsl(q, 2), xs.at[q, 1], xv.at[q, 1], xdev(NX - 1))

    def pp(q, f):
        return rc(fsl(q, f), fsl(q, 4 + f), ps.at[q, f], pv.at[q, f], partner)

    def yc(q):
        return rc(GB.at[q - 2], own(q), ys.at[q - 2], yv.at[q - 2], ydev(NY - q // 2))

    def ya(q):
        return rc(GA.at[q - 2], fsl(q, 3), yas.at[q - 2], yav.at[q - 2], ydev(NY - q // 2))

    def send_own(q):
        xr(q).start()
        xl(q).start()
        pp(q, 0).start()

    @pl.loop(0, 2)
    def _(q):
        place(q)
        for a in range(2):
            RB[q, a, :, 0:FS] = gather(q, a, XB)
        send_own(q)

    @pl.loop(2, Q)
    def _(q):
        e = ((NY - q // 2) % NY) * 2 + q % 2
        place(e)
        for a in range(2):
            GB[q - 2, a] = gather(e, a, XB)
        yc(q).start()

    for cp in wloads:
        cp.wait()
    for d in range(NZ):
        T[d] = jnp.zeros((TOK, FS), F32)

    nt = (((1,), (1,)), ((), ()))
    tn = (((0,), (0,)), ((), ()))

    def px(q):
        return rc(PB.at[q, pl.ds(4, 4)], PX.at[q % 4], pxs.at[q], pxv.at[q], partner)

    def ra(q, w):
        return rc(
            PB.at[q, 3, :, pl.ds(w * (FS // 2), FS // 2)], RA.at[q, w],
            as_.at[q, w], av.at[q, w], xdev(1 if w == 0 else NX - 1),
        )

    def rm(q, w):
        return rc(
            PB.at[q, 2 - w], RM.at[q, w], rs.at[q, w], rv.at[q, w], xdev(1 if w == 0 else NX - 1)
        )

    def ry(q):
        return rc(FB.at[q - 2], YB.at[q], rys.at[q - 2], ryv.at[q - 2], ydev(q // 2))

    def step_a(q):
        yc(q).wait_recv()
        send_own(q)

    def step_b(q):
        xr(q).wait_recv()
        pp(q, 1).start()
        xl(q).wait_recv()
        pp(q, 2).start()

    def step_c(q):
        ya(q).wait_recv()
        pp(q, 3).start()

    def step_d(q):
        j = q % 2
        for f in range(4):
            pp(q, f).wait_recv()
        pre_gate = lax.dot_general(RB[q, 0], WV[j, 0:FFL, :], nt, preferred_element_type=F32)
        pre_up = lax.dot_general(
            RB[q, 0], WV[j, FFL : 2 * FFL, :], nt, preferred_element_type=F32
        )
        hidden = lax.dot_general(
            RB[q, 1], WV[j, 2 * FFL : 3 * FFL, :], nt, preferred_element_type=F32
        )
        sg = jax.nn.sigmoid(pre_gate)
        act = pre_gate * sg
        prod = act * pre_up * hidden
        hi = prod.astype(BF)
        lo = (prod - hi.astype(F32)).astype(BF)
        ones = jnp.ones((8, FFL), BF)
        score = lax.dot_general(ones, hi, nt, preferred_element_type=F32)
        score = score + lax.dot_general(ones, lo, nt, preferred_element_type=F32)
        SC[q, :, 0:R] = score[0:1]
        gpg = (hidden * pre_up * sg * (1.0 + pre_gate * (1.0 - sg))).astype(BF)
        gpu = (hidden * act).astype(BF)
        for f in (4, 5, 6, 7, 3, 2, 1, 0):
            part = jnp.dot(gpg, WV[j, 0:FFL, f * FS : (f + 1) * FS], preferred_element_type=F32)
            part = part + jnp.dot(
                gpu, WV[j, FFL : 2 * FFL, f * FS : (f + 1) * FS], preferred_element_type=F32
            )
            PB[q, f] = part.astype(BF)
            if f == 7:
                px(q).start()

    def step_e(q):
        px(q).wait_recv()
        for f in (3, 2, 1, 0):
            PB[q, f] = (PB[q, f].astype(F32) + PX[q % 4, f].astype(F32)).astype(BF)
            if f == 3:
                ra(q, 0).start()
                ra(q, 1).start()

    def step_f(q):
        for w in range(2):
            ra(q, w).wait_recv()
            lo, hi = w * (FS // 2), (w + 1) * (FS // 2)
            PB[q, 2 - w, :, lo:hi] = (
                PB[q, 2 - w, :, lo:hi].astype(F32) + RA[q, w].astype(F32)
            ).astype(BF)
            rm(q, w).start()

    def step_g(q):
        rm(q, 0).wait_recv()
        rm(q, 1).wait_recv()
        total = PB[q, 0].astype(F32) + RM[q, 0].astype(F32) + RM[q, 1].astype(F32)

        @pl.when(q < 2)
        def _():
            YB[q] = total.astype(BF)

        @pl.when(q >= 2)
        def _():
            FB[q - 2] = total.astype(BF)
            ry(q).start()

    def step_h(q):
        @pl.when(q >= 2)
        def _():
            ry(q).wait_recv()

        e = ((NY - q // 2) % NY) * 2 + q % 2
        for d in range(NZ):
            pick = PLB[e, :, d * TOK : (d + 1) * TOK].astype(F32)
            pick = pick * jnp.broadcast_to(WT[e, :, d * TOK : (d + 1) * TOK], (R, TOK))
            T[d] += lax.dot_general(pick.astype(BF), YB[q], tn, preferred_element_type=F32)

    def scx(k):
        return rc(SC, SCR.at[me_c], scs.at[k - 1], scv.at[k - 1], cdev(k))

    def scy(k):
        return rc(SCT, YSC.at[k - 1], sys_.at[k - 1], syv.at[k - 1], ydev(NY - k))

    def scz(k):
        return rc(SE.at[k], ZSC.at[NZ - k], szs.at[k - 1], szv.at[k - 1], zdev(k))

    def during(q, run):
        pl.when((q >= 0) & (q < Q))(lambda: run(q))

    def ring_a(s):
        for a in range(2):
            for way in range(2):
                if s < half or a == way:
                    za(way, s, a).wait_recv()
                if s + 1 < half or (s + 1 == half and a == way):
                    za(way, s + 1, a).start()

    ring_a(1)
    step_b(0)
    step_a(2)
    ring_a(2)
    step_b(1)
    step_a(3)
    ring_a(3)
    step_a(4)
    ring_a(4)

    @pl.loop(0, 2)
    def _(q):
        for a in range(2):
            RB[q, a, :, 3 * FS : 4 * FS] = gather(q, a, XA)
        pp(q, 3).start()

    @pl.loop(2, Q)
    def _(q):
        e = ((NY - q // 2) % NY) * 2 + q % 2
        for a in range(2):
            GA[q - 2, a] = gather(e, a, XA)
        ya(q).start()

    @pl.loop(0, Q + 4)
    def _(t):
        pl.when(t < Q - 5)(lambda: step_a(t + 5))
        pl.when(t < Q - 2)(lambda: step_b(t + 2))
        pl.when((t >= 1) & (t < Q - 1))(lambda: step_c(t + 1))
        during(t - 1, step_e)
        during(t, step_d)

        @pl.when(t == Q - 1)
        def _():
            for k in range(1, NF):
                scx(k).start()

        during(t - 2, step_f)
        during(t - 3, step_g)
        during(t - 4, step_h)

    hf = FS // 2

    def zt(way, s):
        dev = zdev(1 if way == 0 else NZ - 1)
        if s == 1:
            lanes = pl.ds(way * hf, hf)
            src, dst = ZS.at[way, 0, :, lanes], ZR.at[way, 0, :, lanes]
        else:
            src, dst = ZS.at[way, s - 1], ZR.at[way, s - 1]
        return rc(src, dst, zrs.at[way, s - 1], zrv.at[way, s - 1], dev)

    for way in range(2):
        lanes = slice(way * hf, (way + 1) * hf)
        ZS[way, 0, :, lanes] = T[half, :, lanes].astype(BF)
        zt(way, 1).start()

    SCR[me_c] = SC[...]
    for k in range(1, NF):
        scx(k).wait_recv()
    total = SCR[0]
    for k in range(1, NF):
        total = total + SCR[k]
    SCT[...] = total
    for k in range(1, NY):
        scy(k).start()

    def ring(s):
        for way in range(2):
            zt(way, s - 1).wait_recv()
            d = half - (s - 1) if way == 0 else half + (s - 1)
            if s == 2:
                lanes = slice(way * hf, (way + 1) * hf)
                other = slice((1 - way) * hf, (2 - way) * hf)
                ZS[way, 1, :, lanes] = (
                    T[d, :, lanes] + ZR[way, 0, :, lanes].astype(F32)
                ).astype(BF)
                ZS[way, 1, :, other] = T[d, :, other].astype(BF)
            else:
                ZS[way, s - 1] = (T[d] + ZR[way, s - 2].astype(F32)).astype(BF)
            zt(way, s).start()

    ring(2)
    for dy in range(NY):
        if dy:
            scy(dy).wait_recv()
        for j in range(2):
            e = dy * 2 + j
            row = ((NY - dy) % NY) * 2 + j
            table = SCT[row, :, 0:R] if dy == 0 else YSC[dy - 1, row, :, 0:R]
            table = jnp.broadcast_to(table, (8, R))
            hi = table.astype(BF)
            lo = (table - hi.astype(F32)).astype(BF)
            spread = jnp.dot(hi, PLB[e], preferred_element_type=F32)
            spread = spread + jnp.dot(lo, PLB[e], preferred_element_type=F32)
            for d in range(NZ):
                SE[d, e : e + 1, :] = spread[0:1, d * TOK : (d + 1) * TOK]
    for k in range(1, NZ):
        scz(k).start()
    for s in range(3, half + 1):
        ring(s)

    gates = jnp.zeros((TOP, TOK), F32)
    ids = MB[0, 0:TOP, :]
    for d in range(NZ):
        if d:
            scz(NZ - d).wait_recv()
        piece = SE[0] if d == 0 else ZSC[d]
        for i in range(8):
            who = (2 * (((y + i // 2) % NY) * NZ + (z + d) % NZ) + i % 2).astype(F32)
            gates = gates + jnp.where(
                ids == who, jnp.broadcast_to(piece[i : i + 1, :], (TOP, TOK)), 0.0
            )
    gg[...] = gates.astype(BF)

    for way in range(2):
        zt(way, half).wait_recv()
    out[...] = (
        T[0] + ZR[0, half - 1].astype(F32) + ZR[1, half - 1].astype(F32)
    ).astype(BF)

    for a in range(2):
        xa(a).wait_send()
    for s in range(1, half + 1):
        for way in range(2):
            if s < half or way == 0:
                zm(way, s).wait_send()
            for a in range(2):
                if s < half or a == way:
                    zx(way, s, a).wait_send()
                    za(way, s, a).wait_send()
            zt(way, s).wait_send()

    @pl.loop(0, Q)
    def _(q):
        for cp in (xr(q), xl(q), px(q), ra(q, 0), ra(q, 1), rm(q, 0), rm(q, 1)):
            cp.wait_send()
        for f in range(4):
            pp(q, f).wait_send()

    @pl.loop(2, Q)
    def _(q):
        yc(q).wait_send()
        ya(q).wait_send()
        ry(q).wait_send()

    for k in range(1, NF):
        scx(k).wait_send()
    for k in range(1, NY):
        scy(k).wait_send()
    for k in range(1, NZ):
        scz(k).wait_send()


def body(tokens, grad_out, expert_ids, gate_probs, gate_weight, up_weight, down_weight):
    V, S = pltpu.VMEM, pltpu.SemaphoreType.DMA
    scratch = [
        V((NZ, 2, TOK, FS), BF), V((NZ, 2, TOK, FS), BF), V((NZ, 2 * TOP, TOK), F32),
        V((8, 1, NZ * TOK), F32), V((8, 1, NZ * TOK), F32), V((8, R, NZ * TOK), BF),
        V((Q - 2, 2, R, FS), BF), V((Q - 2, 2, R, FS), BF), V((Q, 2, R, D), BF), V((2, 3 * FFL, D), BF),
        V((Q, NF, R, FS), BF), V((4, 4, R, FS), BF), V((Q, 2, R, FS // 2), BF),
        V((Q, 2, R, FS), BF), V((Q - 2, R, FS), BF), V((Q, R, FS), BF),
        V((NZ, TOK, FS), F32), V((2, NZ // 2, TOK, FS), BF), V((2, NZ // 2, TOK, FS), BF),
        V((Q, 1, 256), F32), V((NF, Q, 1, 256), F32), V((Q, 1, 256), F32),
        V((NY - 1, Q, 1, 256), F32),
        V((NZ, 8, TOK), F32), V((NZ, 8, TOK), F32),
        S((2,)), S((2, NF, 3)),
        S((2, 4, 2)), S((2, 4, 2)), S((2, 4, 2)), S((2, 4, 2)), S((2,)), S((2,)),
        S((2, 4)), S((2, 4)), S((Q - 2,)), S((Q - 2,)), S((Q - 2,)), S((Q - 2,)),
        S((Q, 2)), S((Q, 2)), S((Q, 4)), S((Q, 4)), S((Q,)), S((Q,)),
        S((Q, 2)), S((Q, 2)), S((Q, 2)), S((Q, 2)), S((Q - 2,)), S((Q - 2,)), S((2, 4)), S((2, 4)),
        S((NF - 1,)), S((NF - 1,)), S((NY - 1,)), S((NY - 1,)), S((NZ - 1,)), S((NZ - 1,)),
    ]
    anyspec = pl.BlockSpec(memory_space=pl.ANY)
    vmem = pl.BlockSpec(memory_space=pltpu.VMEM)
    out, gates = pl.pallas_call(
        kernel,
        out_shape=(
            jax.ShapeDtypeStruct((TOK, FS), BF),
            jax.ShapeDtypeStruct((TOP, TOK), BF),
        ),
        in_specs=[anyspec] * 2 + [vmem] * 2 + [anyspec] * 3,
        out_specs=(vmem, vmem),
        scratch_shapes=scratch,
        compiler_params=pltpu.CompilerParams(
            collective_id=0, has_side_effects=True, vmem_limit_bytes=60 * 1024 * 1024
        ),
        name="expert_grad",
    )(tokens, grad_out, expert_ids.T, gate_probs.T, gate_weight, up_weight, down_weight)
    return out, gates.T


def solution(mesh):
    in_specs = (
        P("expert", "ctx"),
        P("expert", "ctx"),
        P("expert", None),
        P("expert", None),
        P("expert", "ctx", None),
        P("expert", "ctx", None),
        P("expert", "ctx", None),
    )
    out_specs = (P("expert", "ctx"), P("expert", None))
    return jax.shard_map(body, mesh=mesh, in_specs=in_specs, out_specs=out_specs, check_vma=False)
```

```python
import jax
import jax.numpy as jnp
from jax import lax
from jax.experimental import pallas as pl
from jax.experimental.pallas import tpu as pltpu
from jax.sharding import PartitionSpec as P

MESH = pl.DeviceIdType.MESH
NY, NZ, NX = 4, 8, 4
CAP, TOK, TOP = 18, 128, 8
R = NZ * CAP
FS, FFL, NF = 512, 192, 8
D = FS * NF
Q = NY
U = 2 * NY - 1
BF, F32 = jnp.bfloat16, jnp.float32
POS = (0, 1, 3, 5, 7, 6, 4, 2)
NEAR = ((0, 48, 0, 3), (48, 32, 2, 5), (80, 64, 4, 8))
FAR = ((0, 80, 0, 5), (80, 64, 4, 8))


def rc(src, dst, ss, rs, dev):
    return pltpu.make_async_remote_copy(
        src_ref=src, dst_ref=dst, send_sem=ss, recv_sem=rs, device_id=dev, device_id_type=MESH
    )


def kernel(
    tok, grad, ids_in, probs_in, wg, wu, wd, out, gg,
    XB, XA, MB, KEY, WT, PLB, GB, GA, RB, WV, PB, RM, FB, YB, YF, T, TF, ZS, ZR, ZSF, ZRF, OS, OR,
    SC, SCR, SCT, YSC, SE, ZSC,
    ls, ws, wrs, wrv, zs, zv, zas, zav, xas, xav, ms, mv, ys, yv, yas, yav, xs, xv,
    fys, fyv, rs, rv, rys, ryv, zrs, zrv, fzs, fzv, os_, ov, scs, scv, sys_, syv, szs, szv,
):
    me_e, me_c = lax.axis_index("expert"), lax.axis_index("ctx")
    y, z = me_e // NZ, me_e % NZ
    x, c = me_c // 2, me_c % 2

    def xdev(dx):
        return {"ctx": ((x + dx) % NX) * 2 + c}

    partner = {"ctx": x * 2 + 1 - c}

    def ydev(dy):
        return {"expert": ((y + dy) % NY) * NZ + z}

    def zdev(dz):
        return {"expert": y * NZ + (z + dz) % NZ}

    def cdev(k):
        return {"ctx": (me_c + k) % NF}

    loads = [
        pltpu.make_async_copy(tok, XB.at[0, 0], ls.at[0]),
        pltpu.make_async_copy(grad, XB.at[0, 1], ls.at[1]),
    ]
    for cp in loads:
        cp.start()

    MB[0, 0:TOP, :] = ids_in[...].astype(F32)
    MB[0, TOP : 2 * TOP, :] = probs_in[...]

    barrier = pltpu.get_barrier_semaphore()
    peers = [cdev(k) for k in range(1, NF)] + [ydev(k) for k in range(1, NY)]
    peers += [zdev(k) for k in range(1, NZ)]
    peers += [{**ydev(k), **partner} for k in range(1, NY)]
    for peer in peers:
        pl.semaphore_signal(barrier, inc=1, device_id=peer, device_id_type=MESH)
    pl.semaphore_wait(barrier, len(peers))
    for cp in loads:
        cp.wait()

    def zx(way, s, a):
        if way == 0:
            si, di, dev = (NZ - (s - 1)) % NZ, NZ - s, zdev(1)
        else:
            si, di, dev = s - 1, s, zdev(NZ - 1)
        si, di = POS[si], POS[di]
        return rc(XB.at[si, a], XB.at[di, a], zs.at[way, s - 1, a], zv.at[way, s - 1, a], dev)

    def za(way, s, a):
        if way == 0:
            si, di, dev = (NZ - (s - 1)) % NZ, NZ - s, zdev(1)
        else:
            si, di, dev = s - 1, s, zdev(NZ - 1)
        si, di = POS[si], POS[di]
        return rc(XA.at[si, a], XA.at[di, a], zas.at[way, s - 1, a], zav.at[way, s - 1, a], dev)

    def xa(a):
        return rc(XB.at[0, a], XA.at[0, a], xas.at[a], xav.at[a], xdev(2))

    def zm(way, s):
        if way == 0:
            si, di, dev = (NZ - (s - 1)) % NZ, NZ - s, zdev(1)
        else:
            si, di, dev = s - 1, s, zdev(NZ - 1)
        return rc(MB.at[si], MB.at[di], ms.at[way, s - 1], mv.at[way, s - 1], dev)

    lane = lax.broadcasted_iota(jnp.int32, (TOK, TOK), 1)
    sub = lax.broadcasted_iota(jnp.int32, (TOK, TOK), 0)
    before = (sub < lane).astype(BF)
    erow = lax.broadcasted_iota(jnp.int32, (8, TOK), 0)
    dyrow = erow // 2
    expert = (2 * (((y + dyrow) % NY) * NZ + z) + (erow - 2 * dyrow)).astype(F32)

    def key(d):
        member = jnp.zeros((8, TOK), F32)
        weight = jnp.zeros((8, TOK), F32)
        for k in range(TOP):
            hit = jnp.broadcast_to(MB[d, k : k + 1, :], (8, TOK)) == expert
            member = member + jnp.where(hit, 1.0, 0.0)
            prob = jnp.broadcast_to(MB[d, TOP + k : TOP + k + 1, :], (8, TOK))
            weight = weight + jnp.where(hit, prob, 0.0)
        rank = jnp.dot(member.astype(BF), before, preferred_element_type=F32)
        p = POS[d]
        slot = jnp.where(member > 0.5, rank + float(p * CAP), -1.0)
        for e in range(8):
            KEY[e, :, p * TOK : (p + 1) * TOK] = slot[e : e + 1]
            WT[e, :, p * TOK : (p + 1) * TOK] = weight[e : e + 1]

    half = NZ // 2
    for way in range(2):
        zm(way, 1).start()
    for a in range(2):
        for way in range(2):
            zx(way, 1, a).start()
    for a in range(2):
        xa(a).start()

    def wslice(m, f, expert_of):
        xo = (0, NX - 1, 1, 2)[f // 2]
        ctx = ((x + xo) % NX) * 2 + f % 2
        src = (wg, wu, wd)[m].at[expert_of, :, pl.ds(pl.multiple_of(ctx * FS, FS), FS)]
        rows = pl.ds(pl.multiple_of(c * FFL, FFL), FFL)
        return src, WV.at[m, rows, pl.ds(f * FS, FS)]

    def wload(m, f):
        return pltpu.make_async_copy(*wslice(m, f, c), ws.at[m, f])

    def wgive(m, f):
        return rc(*wslice(m, f, 1 - c), wrs.at[m, f], wrv.at[m, f], partner)

    for m in range(3):
        for f in range(NF):
            wgive(m, f).start()
            wload(m, f).start()

    @pl.loop(0, 8)
    def _(e):
        PLB[e] = jnp.zeros((R, NZ * TOK), BF)

    def place(e, part):
        r0, n, p0, p1 = part
        rowid = lax.broadcasted_iota(jnp.int32, (n, (p1 - p0) * TOK), 0).astype(F32) + float(r0)
        keys = jnp.broadcast_to(KEY[e, :, p0 * TOK : p1 * TOK], (n, (p1 - p0) * TOK))
        PLB[e, r0 : r0 + n, p0 * TOK : p1 * TOK] = jnp.where(keys == rowid, 1.0, 0.0).astype(BF)

    def gather(e, a, slabs, part):
        r0, n, p0, p1 = part
        slab = slabs[p0:p1, a].reshape((p1 - p0) * TOK, FS)
        pick = PLB[e, r0 : r0 + n, p0 * TOK : p1 * TOK]
        return jnp.dot(pick, slab, preferred_element_type=F32).astype(BF)

    def fsl(q, f, part):
        lanes = pl.ds(pl.multiple_of(f * FS, FS), FS)
        return RB.at[q, :, pl.ds(part[0], part[1]), lanes]

    def pair(u):
        return (u + 1) // 2, (u + 1) % 2

    def ydst(u):
        q, j = pair(u)
        return {"expert": ((y + NY - q) % NY) * NZ + z, "ctx": x * 2 + j}

    def rows(buf, u, part):
        return buf.at[u, :, pl.ds(part[0], part[1])]

    def yc(u, k):
        return rc(
            rows(GB, u, NEAR[k]), fsl(pair(u)[0], c, NEAR[k]),
            ys.at[k, u], yv.at[k, pair(u)[0], c], ydst(u),
        )

    def ya(u, k):
        return rc(
            rows(GA, u, FAR[k]), fsl(pair(u)[0], 6 + c, FAR[k]),
            yas.at[k, u], yav.at[k, pair(u)[0], c], ydst(u),
        )

    def pc(k):
        return rc(rows(GB, 0, NEAR[k]), fsl(0, c, NEAR[k]), ys.at[k, 0], yv.at[k, 0, c], partner)

    def pa(k):
        return rc(rows(GA, 0, FAR[k]), fsl(0, 6 + c, FAR[k]), yas.at[k, 0], yav.at[k, 0, c], partner)

    def got(q, cs, k):
        part = NEAR[k]
        return rc(rows(GB, 0, part), fsl(q, cs, part), ys.at[k, 0], yv.at[k, q, cs], partner)

    def got_a(q, cs, k):
        part = FAR[k]
        return rc(rows(GA, 0, part), fsl(q, 6 + cs, part), yas.at[k, 0], yav.at[k, q, cs], partner)

    def xw(q, cs, w, k):
        dev = xdev(1 if w == 0 else NX - 1)
        return rc(
            fsl(q, cs, NEAR[k]), fsl(q, 2 + 2 * w + cs, NEAR[k]),
            xs.at[k, q, w, cs], xv.at[k, q, w, cs], dev,
        )

    def send_x(q, cs, k):
        xw(q, cs, 0, k).start()
        xw(q, cs, 1, k).start()

    def step_a(k):
        @pl.loop(1, Q)
        def _(q):
            for cs in range(2):
                got(q, cs, k).wait_recv()
                send_x(q, cs, k)

    lanes_own = pl.ds(pl.multiple_of(c * FS, FS), FS)
    lanes_far = pl.ds(pl.multiple_of((6 + c) * FS, FS), FS)

    def near(k):
        part = NEAR[k]
        r0, r1 = part[0], part[0] + part[1]
        place(c, part)
        for a in range(2):
            RB[0, a, r0:r1, lanes_own] = gather(c, a, XB, part)
        send_x(0, c, k)
        place(1 - c, part)
        for a in range(2):
            GB[0, a, r0:r1] = gather(1 - c, a, XB, part)
        pc(k).start()

        @pl.loop(1, U)
        def _(u):
            q, j = pair(u)
            e = ((NY - q) % NY) * 2 + j
            place(e, part)
            for a in range(2):
                GB[u, a, r0:r1] = gather(e, a, XB, part)
            yc(u, k).start()

        got(0, 1 - c, k).wait_recv()
        send_x(0, 1 - c, k)

    def far(k):
        part = FAR[k]
        r0, r1 = part[0], part[0] + part[1]

        @pl.loop(1, U)
        def _(u):
            q, j = pair(u)
            e = ((NY - q) % NY) * 2 + j
            for a in range(2):
                GA[u, a, r0:r1] = gather(e, a, XA, part)
            ya(u, k).start()

        for a in range(2):
            GA[0, a, r0:r1] = gather(1 - c, a, XA, part)
        pa(k).start()
        for a in range(2):
            RB[0, a, r0:r1, lanes_far] = gather(c, a, XA, part)

    def ring_a(s):
        for a in range(2):
            for way in range(2):
                if s < half or a == way:
                    za(way, s, a).wait_recv()
                if s + 1 < half or (s + 1 == half and a == way):
                    za(way, s + 1, a).start()

    key(0)
    for d in range(NZ):
        T[d] = jnp.zeros((TOK, FS), F32)
        TF[d] = jnp.zeros((TOK, FS), F32)
    for s in range(1, half + 1):
        for way in range(2):
            if s < half or way == 0:
                zm(way, s).wait_recv()
                if s + 1 < half or (s + 1 == half and way == 0):
                    zm(way, s + 1).start()
        key(NZ - s)
        if s < half:
            key(s)
        for a in range(2):
            for way in range(2):
                if s < half or a == way:
                    zx(way, s, a).wait_recv()
                if s + 1 < half or (s + 1 == half and a == way):
                    zx(way, s + 1, a).start()
        if s == 1:
            near(0)
        elif s == 2:
            near(1)
        elif s == half - 1:
            for a in range(2):
                xa(a).wait_recv()
                for way in range(2):
                    za(way, 1, a).start()
            step_a(0)
        else:
            near(2)
    step_a(1)
    ring_a(1)
    ring_a(2)
    far(0)
    step_a(2)
    ring_a(3)
    ring_a(4)
    far(1)
    for m in range(3):
        for f in range(NF):
            wload(m, f).wait()
            wgive(m, f).wait_recv()

    nt = (((1,), (1,)), ((), ()))
    tn = (((0,), (0,)), ((), ()))

    def rm(q, w, cs):
        return rc(
            PB.at[q, 4 - 2 * w + cs], RM.at[q, w, cs], rs.at[q, w, cs], rv.at[q, w, cs],
            xdev(1 if w == 0 else NX - 1),
        )

    def ry(q, cs):
        dev = {"expert": ((y + q) % NY) * NZ + z, "ctx": x * 2 + cs}
        return rc(FB.at[q, cs], YB.at[q, c], rys.at[q, cs], ryv.at[q, c], dev)

    def fy(q, cs):
        dev = {"expert": ((y + q) % NY) * NZ + z, "ctx": x * 2 + cs}
        return rc(PB.at[q, 6 + cs], YF.at[q, c], fys.at[q, cs], fyv.at[q, c], dev)

    def fy_got(q, j):
        return rc(PB.at[q, 6], YF.at[q, j], fys.at[q, 0], fyv.at[q, j], partner)

    def ry_got(q, j):
        return rc(FB.at[q, 0], YB.at[q, j], rys.at[q, 0], ryv.at[q, j], partner)

    def step_d(q):
        for k in range(3):
            for cs in range(2):
                xw(q, cs, 0, k).wait_recv()
                xw(q, cs, 1, k).wait_recv()

        def own_far():
            got_a(q, c, 0).wait_recv()
            got_a(q, c, 1).wait_recv()

        got_a(q, 1 - c, 0).wait_recv()
        got_a(q, 1 - c, 1).wait_recv()
        pl.when(q > 0)(own_far)
        gate_up = WV[0:2].reshape(4 * FFL, D)
        pre = lax.dot_general(RB[q, 0], gate_up, nt, preferred_element_type=F32)
        hidden = lax.dot_general(RB[q, 1], WV[2], nt, preferred_element_type=F32)
        pre_gate, pre_up = pre[:, 0 : 2 * FFL], pre[:, 2 * FFL :]
        sg = jax.nn.sigmoid(pre_gate)
        act = pre_gate * sg
        prod = act * pre_up * hidden
        hi = prod.astype(BF)
        lo = (prod - hi.astype(F32)).astype(BF)
        ones = jnp.ones((8, 2 * FFL), BF)
        score = lax.dot_general(ones, hi, nt, preferred_element_type=F32)
        score = score + lax.dot_general(ones, lo, nt, preferred_element_type=F32)
        SC[q, :, 0:R] = score[0:1]
        gpg = (hidden * pre_up * sg * (1.0 + pre_gate * (1.0 - sg))).astype(BF)
        gpu = (hidden * act).astype(BF)
        both = jnp.concatenate([gpg, gpu], axis=1)
        for f in (6, 7, 4, 2, 5, 3, 0, 1):
            weights = WV[0:2, :, f * FS : (f + 1) * FS].reshape(4 * FFL, FS)
            PB[q, f] = jnp.dot(both, weights, preferred_element_type=F32).astype(BF)
            if f >= 6:
                cs = f - 6
                pl.when((q > 0) | (c != cs))(lambda: fy(q, cs).start())
            elif f >= 2:
                rm(q, 0 if f >= 4 else 1, f % 2).start()

    def step_g(q):
        def total(cs):
            for w in range(2):
                rm(q, w, cs).wait_recv()
            near = PB[q, cs].astype(F32) + RM[q, 0, cs].astype(F32)
            return (near + RM[q, 1, cs].astype(F32)).astype(BF)

        for cs in range(2):
            FB[q, cs] = total(cs)
            pl.when((q > 0) | (c != cs))(lambda: ry(q, cs).start())

    def combine(q, rows_of, sums):
        e0 = ((NY - q) % NY) * 2
        for j in range(2):
            for d in range(NZ):
                pick = PLB[e0 + j, :, d * TOK : (d + 1) * TOK].astype(F32)
                weight = WT[e0 + j, :, d * TOK : (d + 1) * TOK]
                pick = pick * jnp.broadcast_to(weight, (R, TOK))
                sums[d] += lax.dot_general(
                    pick.astype(BF), rows_of[q, j], tn, preferred_element_type=F32
                )

    def step_h(q):
        for j in range(2):
            pl.when((q > 0) | (c != j))(lambda: ry_got(q, j).wait_recv())

        @pl.when(q == 0)
        def _():
            YB[0, c] = FB[0, c]

        combine(q, YB, T)

    def step_hf(q):
        for j in range(2):
            pl.when((q > 0) | (c != j))(lambda: fy_got(q, j).wait_recv())

        @pl.when(q == 0)
        def _():
            YF[0, c] = PB[0, 6 + c]

        combine(q, YF, TF)

    def scx(k):
        return rc(SC, SCR.at[me_c], scs.at[k - 1], scv.at[k - 1], cdev(k))

    def scy(k):
        return rc(SCT, YSC.at[k - 1], sys_.at[k - 1], syv.at[k - 1], ydev(NY - k))

    def scz(k):
        return rc(SE.at[k], ZSC.at[NZ - k], szs.at[k - 1], szv.at[k - 1], zdev(k))

    hf = FS // 2

    class Ring:
        def __init__(self, sums, sent, came, ss, rs):
            self.sums, self.sent, self.came, self.ss, self.rs = sums, sent, came, ss, rs

        def copy(self, way, s, p):
            lanes = pl.ds(p * hf, hf)
            return rc(
                self.sent.at[way, s - 1, :, lanes], self.came.at[way, s - 1, :, lanes],
                self.ss.at[way, s - 1, p], self.rs.at[way, s - 1, p],
                zdev(1 if way == 0 else NZ - 1),
            )

        def hop(self, way, s, p):
            d = half - (s - 1) if way == 0 else half + (s - 1)
            lanes = slice(p * hf, (p + 1) * hf)
            value = self.sums[POS[d], :, lanes]
            if s > 2 or (s == 2 and p == way):
                self.copy(way, s - 1, p).wait_recv()
                value = value + self.came[way, s - 2, :, lanes].astype(F32)
            self.sent[way, s - 1, :, lanes] = value.astype(BF)
            self.copy(way, s, p).start()

        def begin(self):
            for way in range(2):
                self.hop(way, 1, way)
            for way in range(2):
                self.hop(way, 2, 1 - way)

        def step(self, s):
            for way in range(2):
                self.hop(way, s, way)
            if s > 2:
                for way in range(2):
                    self.hop(way, s, 1 - way)

        def result(self, p):
            lanes = slice(p * hf, (p + 1) * hf)
            value = self.sums[0, :, lanes]
            for way in range(2):
                self.copy(way, half, p).wait_recv()
                value = value + self.came[way, half - 1, :, lanes].astype(F32)
            return value

    near_ring = Ring(T, ZS, ZR, zrs, zrv)
    far_ring = Ring(TF, ZSF, ZRF, fzs, fzv)

    def swap():
        return rc(OS, OR, os_, ov, xdev(2))

    pl.loop(0, Q)(step_d)
    for k in range(1, NF):
        scx(k).start()
    pl.loop(0, Q)(step_hf)
    far_ring.begin()
    step_g(0)
    far_ring.step(2)
    step_g(1)
    far_ring.step(3)
    step_g(2)
    far_ring.step(4)

    SCR[me_c] = SC[...]
    for k in range(1, NF):
        scx(k).wait_recv()
    for j in range(2):
        total = SCR[j]
        for k in range(1, NX):
            total = total + SCR[2 * k + j]
        SCT[j] = total
    for k in range(1, NY):
        scy(k).start()

    step_g(3)
    pl.loop(0, Q - 1)(step_h)
    for p in range(2):
        OS[:, p * hf : (p + 1) * hf] = far_ring.result(p).astype(BF)
    swap().start()
    step_h(Q - 1)
    near_ring.begin()
    near_ring.step(2)
    for dy in range(NY):
        if dy:
            scy(dy).wait_recv()
        for j in range(2):
            e = dy * 2 + j
            row = (NY - dy) % NY
            table = SCT[j, row, :, 0:R] if dy == 0 else YSC[dy - 1, j, row, :, 0:R]
            table = jnp.broadcast_to(table, (8, R))
            hi = table.astype(BF)
            lo = (table - hi.astype(F32)).astype(BF)
            spread = jnp.dot(hi, PLB[e], preferred_element_type=F32)
            spread = spread + jnp.dot(lo, PLB[e], preferred_element_type=F32)
            for d in range(NZ):
                SE[d, e : e + 1, :] = spread[0:1, POS[d] * TOK : (POS[d] + 1) * TOK]
    for k in range(1, NZ):
        scz(k).start()
    for s in range(3, half + 1):
        near_ring.step(s)

    gates = jnp.zeros((TOP, TOK), F32)
    ids = MB[0, 0:TOP, :]
    for d in range(NZ):
        if d:
            scz(NZ - d).wait_recv()
        piece = SE[0] if d == 0 else ZSC[d]
        for i in range(8):
            who = (2 * (((y + i // 2) % NY) * NZ + (z + d) % NZ) + i % 2).astype(F32)
            gates = gates + jnp.where(
                ids == who, jnp.broadcast_to(piece[i : i + 1, :], (TOP, TOK)), 0.0
            )
    gg[...] = gates.astype(BF)

    swap().wait_recv()
    for p in range(2):
        lanes = slice(p * hf, (p + 1) * hf)
        out[:, lanes] = (near_ring.result(p) + OR[:, lanes].astype(F32)).astype(BF)

    for m in range(3):
        for f in range(NF):
            wgive(m, f).wait_send()
    for a in range(2):
        xa(a).wait_send()
    for s in range(1, half + 1):
        for way in range(2):
            if s < half or way == 0:
                zm(way, s).wait_send()
            for a in range(2):
                if s < half or a == way:
                    zx(way, s, a).wait_send()
                    za(way, s, a).wait_send()
                if s > 1 or a == way:
                    near_ring.copy(way, s, a).wait_send()
                    far_ring.copy(way, s, a).wait_send()

    @pl.loop(0, Q)
    def _(q):
        for w in range(2):
            for cs in range(2):
                for k in range(3):
                    xw(q, cs, w, k).wait_send()
                rm(q, w, cs).wait_send()
        for cs in range(2):
            pl.when((q > 0) | (c != cs))(lambda: ry(q, cs).wait_send())
            pl.when((q > 0) | (c != cs))(lambda: fy(q, cs).wait_send())

    swap().wait_send()
    for k in range(3):
        pc(k).wait_send()
    for k in range(2):
        pa(k).wait_send()

    @pl.loop(1, U)
    def _(u):
        for k in range(3):
            yc(u, k).wait_send()
        for k in range(2):
            ya(u, k).wait_send()

    for k in range(1, NF):
        scx(k).wait_send()
    for k in range(1, NY):
        scy(k).wait_send()
    for k in range(1, NZ):
        scz(k).wait_send()


def body(tokens, grad_out, expert_ids, gate_probs, gate_weight, up_weight, down_weight):
    V, S = pltpu.VMEM, pltpu.SemaphoreType.DMA
    scratch = [
        V((NZ, 2, TOK, FS), BF), V((NZ, 2, TOK, FS), BF), V((NZ, 2 * TOP, TOK), F32),
        V((8, 1, NZ * TOK), F32), V((8, 1, NZ * TOK), F32), V((8, R, NZ * TOK), BF),
        V((U, 2, R, FS), BF), V((U, 2, R, FS), BF), V((Q, 2, R, D), BF), V((3, 2 * FFL, D), BF),
        V((Q, NF, R, FS), BF), V((Q, 2, 2, R, FS), BF),
        V((Q, 2, R, FS), BF), V((Q, 2, R, FS), BF), V((Q, 2, R, FS), BF),
        V((NZ, TOK, FS), F32), V((NZ, TOK, FS), F32),
        V((2, NZ // 2, TOK, FS), BF), V((2, NZ // 2, TOK, FS), BF),
        V((2, NZ // 2, TOK, FS), BF), V((2, NZ // 2, TOK, FS), BF),
        V((TOK, FS), BF), V((TOK, FS), BF),
        V((Q, 1, 256), F32), V((NF, Q, 1, 256), F32), V((2, Q, 1, 256), F32),
        V((NY - 1, 2, Q, 1, 256), F32), V((NZ, 8, TOK), F32), V((NZ, 8, TOK), F32),
        S((2,)), S((3, NF)), S((3, NF)), S((3, NF)),
        S((2, 4, 2)), S((2, 4, 2)), S((2, 4, 2)), S((2, 4, 2)), S((2,)), S((2,)),
        S((2, 4)), S((2, 4)), S((3, U)), S((3, Q, 2)), S((2, U)), S((2, Q, 2)),
        S((3, Q, 2, 2)), S((3, Q, 2, 2)),
        S((Q, 2)), S((Q, 2)), S((Q, 2, 2)), S((Q, 2, 2)), S((Q, 2)), S((Q, 2)),
        S((2, 4, 2)), S((2, 4, 2)), S((2, 4, 2)), S((2, 4, 2)), S(()), S(()),
        S((NF - 1,)), S((NF - 1,)), S((NY - 1,)), S((NY - 1,)), S((NZ - 1,)), S((NZ - 1,)),
    ]
    anyspec = pl.BlockSpec(memory_space=pl.ANY)
    vmem = pl.BlockSpec(memory_space=pltpu.VMEM)
    out, gates = pl.pallas_call(
        kernel,
        out_shape=(
            jax.ShapeDtypeStruct((TOK, FS), BF),
            jax.ShapeDtypeStruct((TOP, TOK), BF),
        ),
        in_specs=[anyspec] * 2 + [vmem] * 2 + [anyspec] * 3,
        out_specs=(vmem, vmem),
        scratch_shapes=scratch,
        compiler_params=pltpu.CompilerParams(
            collective_id=0, has_side_effects=True, vmem_limit_bytes=60 * 1024 * 1024
        ),
        name="expert_grad",
    )(tokens, grad_out, expert_ids.T, gate_probs.T, gate_weight, up_weight, down_weight)
    return out, gates.T


def solution(mesh):
    in_specs = (
        P("expert", "ctx"),
        P("expert", "ctx"),
        P("expert", None),
        P("expert", None),
        P("expert", "ctx", None),
        P("expert", "ctx", None),
        P("expert", "ctx", None),
    )
    out_specs = (P("expert", "ctx"), P("expert", None))
    return jax.shard_map(body, mesh=mesh, in_specs=in_specs, out_specs=out_specs, check_vma=False)
```

```python
import jax
import jax.numpy as jnp
from jax import lax
from jax.experimental import pallas as pl
from jax.experimental.pallas import tpu as pltpu
from jax.sharding import PartitionSpec as P

MESH = pl.DeviceIdType.MESH
NY, NZ, NX = 4, 8, 4
CAP, TOK, TOP = 18, 128, 8
R = NZ * CAP
FS, FFL, NF = 512, 192, 8
D = FS * NF
Q = NY
U = 2 * NY - 1
BF, F32 = jnp.bfloat16, jnp.float32
POS = (0, 1, 3, 5, 7, 6, 4, 2)
NEAR = ((0, 48, 0, 3), (48, 32, 2, 5), (80, 64, 4, 8))
FAR = ((0, 80, 0, 5), (80, 64, 4, 8))


def rc(src, dst, ss, rs, dev):
    return pltpu.make_async_remote_copy(
        src_ref=src, dst_ref=dst, send_sem=ss, recv_sem=rs, device_id=dev, device_id_type=MESH
    )


def kernel(
    tok, grad, ids_in, probs_in, wg, wu, wd, out, gg,
    XB, XA, MB, KEY, WT, PLB, GB, GA, RB, WV, PB, RM, FB, YB, YF, T, TF, ZS, ZR, ZSF, ZRF, OS, OR,
    SC, SCR, SCT, YSC, SE, ZSC,
    ls, ws, wrs, wrv, zs, zv, zas, zav, xas, xav, ms, mv, ys, yv, yas, yav, xs, xv,
    fys, fyv, rs, rv, rys, ryv, zrs, zrv, fzs, fzv, os_, ov, scs, scv, sys_, syv, szs, szv,
):
    me_e, me_c = lax.axis_index("expert"), lax.axis_index("ctx")
    y, z = me_e // NZ, me_e % NZ
    x, c = me_c // 2, me_c % 2

    def xdev(dx):
        return {"ctx": ((x + dx) % NX) * 2 + c}

    partner = {"ctx": x * 2 + 1 - c}

    def ydev(dy):
        return {"expert": ((y + dy) % NY) * NZ + z}

    def zdev(dz):
        return {"expert": y * NZ + (z + dz) % NZ}

    def cdev(k):
        return {"ctx": (me_c + k) % NF}

    loads = [
        pltpu.make_async_copy(tok, XB.at[0, 0], ls.at[0]),
        pltpu.make_async_copy(grad, XB.at[0, 1], ls.at[1]),
    ]
    for cp in loads:
        cp.start()

    MB[0, 0:TOP, :] = ids_in[...].astype(F32)
    MB[0, TOP : 2 * TOP, :] = probs_in[...]

    barrier = pltpu.get_barrier_semaphore()
    peers = [cdev(k) for k in range(1, NF)] + [ydev(k) for k in range(1, NY)]
    peers += [zdev(k) for k in range(1, NZ)]
    peers += [{**ydev(k), **partner} for k in range(1, NY)]
    for peer in peers:
        pl.semaphore_signal(barrier, inc=1, device_id=peer, device_id_type=MESH)
    pl.semaphore_wait(barrier, len(peers))
    for cp in loads:
        cp.wait()

    def zx(way, s, a):
        if way == 0:
            si, di, dev = (NZ - (s - 1)) % NZ, NZ - s, zdev(1)
        else:
            si, di, dev = s - 1, s, zdev(NZ - 1)
        si, di = POS[si], POS[di]
        return rc(XB.at[si, a], XB.at[di, a], zs.at[way, s - 1, a], zv.at[way, s - 1, a], dev)

    def za(way, s, a):
        if way == 0:
            si, di, dev = (NZ - (s - 1)) % NZ, NZ - s, zdev(1)
        else:
            si, di, dev = s - 1, s, zdev(NZ - 1)
        si, di = POS[si], POS[di]
        return rc(XA.at[si, a], XA.at[di, a], zas.at[way, s - 1, a], zav.at[way, s - 1, a], dev)

    def xa(a):
        return rc(XB.at[0, a], XA.at[0, a], xas.at[a], xav.at[a], xdev(2))

    def zm(way, s):
        if way == 0:
            si, di, dev = (NZ - (s - 1)) % NZ, NZ - s, zdev(1)
        else:
            si, di, dev = s - 1, s, zdev(NZ - 1)
        return rc(MB.at[si], MB.at[di], ms.at[way, s - 1], mv.at[way, s - 1], dev)

    lane = lax.broadcasted_iota(jnp.int32, (TOK, TOK), 1)
    sub = lax.broadcasted_iota(jnp.int32, (TOK, TOK), 0)
    before = (sub < lane).astype(BF)
    erow = lax.broadcasted_iota(jnp.int32, (8, TOK), 0)
    dyrow = erow // 2
    expert = (2 * (((y + dyrow) % NY) * NZ + z) + (erow - 2 * dyrow)).astype(F32)

    def key(d):
        member = jnp.zeros((8, TOK), F32)
        weight = jnp.zeros((8, TOK), F32)
        for k in range(TOP):
            hit = jnp.broadcast_to(MB[d, k : k + 1, :], (8, TOK)) == expert
            member = member + jnp.where(hit, 1.0, 0.0)
            prob = jnp.broadcast_to(MB[d, TOP + k : TOP + k + 1, :], (8, TOK))
            weight = weight + jnp.where(hit, prob, 0.0)
        rank = jnp.dot(member.astype(BF), before, preferred_element_type=F32)
        p = POS[d]
        slot = jnp.where(member > 0.5, rank + float(p * CAP), -1.0)
        for e in range(8):
            KEY[e, :, p * TOK : (p + 1) * TOK] = slot[e : e + 1]
            WT[e, :, p * TOK : (p + 1) * TOK] = weight[e : e + 1]

    half = NZ // 2
    for way in range(2):
        zm(way, 1).start()
    for a in range(2):
        for way in range(2):
            zx(way, 1, a).start()
    for a in range(2):
        xa(a).start()

    def wslice(m, f, expert_of):
        xo = (0, NX - 1, 1, 2)[f // 2]
        ctx = ((x + xo) % NX) * 2 + f % 2
        src = (wg, wu, wd)[m].at[expert_of, :, pl.ds(pl.multiple_of(ctx * FS, FS), FS)]
        rows = pl.ds(pl.multiple_of(c * FFL, FFL), FFL)
        return src, WV.at[m, rows, pl.ds(f * FS, FS)]

    def wload(m, f):
        return pltpu.make_async_copy(*wslice(m, f, c), ws.at[m, f])

    def wgive(m, f):
        return rc(*wslice(m, f, 1 - c), wrs.at[m, f], wrv.at[m, f], partner)

    for m in range(3):
        for f in range(NF):
            wgive(m, f).start()
            wload(m, f).start()

    @pl.loop(0, 8)
    def _(e):
        PLB[e] = jnp.zeros((R, NZ * TOK), BF)

    def place(e, part):
        r0, n, p0, p1 = part
        rowid = lax.broadcasted_iota(jnp.int32, (n, (p1 - p0) * TOK), 0).astype(F32) + float(r0)
        keys = jnp.broadcast_to(KEY[e, :, p0 * TOK : p1 * TOK], (n, (p1 - p0) * TOK))
        PLB[e, r0 : r0 + n, p0 * TOK : p1 * TOK] = jnp.where(keys == rowid, 1.0, 0.0).astype(BF)

    def gather(e, a, slabs, part):
        r0, n, p0, p1 = part
        slab = slabs[p0:p1, a].reshape((p1 - p0) * TOK, FS)
        pick = PLB[e, r0 : r0 + n, p0 * TOK : p1 * TOK]
        return jnp.dot(pick, slab, preferred_element_type=F32).astype(BF)

    def fsl(q, f, part):
        lanes = pl.ds(pl.multiple_of(f * FS, FS), FS)
        return RB.at[q, :, pl.ds(part[0], part[1]), lanes]

    def pair(u):
        return (u + 1) // 2, (u + 1) % 2

    def ydst(u):
        q, j = pair(u)
        return {"expert": ((y + NY - q) % NY) * NZ + z, "ctx": x * 2 + j}

    def rows(buf, u, part):
        return buf.at[u, :, pl.ds(part[0], part[1])]

    def yc(u, k):
        return rc(
            rows(GB, u, NEAR[k]), fsl(pair(u)[0], c, NEAR[k]),
            ys.at[k, u], yv.at[k, pair(u)[0], c], ydst(u),
        )

    def ya(u, k):
        return rc(
            rows(GA, u, FAR[k]), fsl(pair(u)[0], 6 + c, FAR[k]),
            yas.at[k, u], yav.at[k, pair(u)[0], c], ydst(u),
        )

    def pc(k):
        return rc(rows(GB, 0, NEAR[k]), fsl(0, c, NEAR[k]), ys.at[k, 0], yv.at[k, 0, c], partner)

    def pa(k):
        return rc(rows(GA, 0, FAR[k]), fsl(0, 6 + c, FAR[k]), yas.at[k, 0], yav.at[k, 0, c], partner)

    def got(q, cs, k):
        part = NEAR[k]
        return rc(rows(GB, 0, part), fsl(q, cs, part), ys.at[k, 0], yv.at[k, q, cs], partner)

    def got_a(q, cs, k):
        part = FAR[k]
        return rc(rows(GA, 0, part), fsl(q, 6 + cs, part), yas.at[k, 0], yav.at[k, q, cs], partner)

    def xw(q, cs, w, k):
        dev = xdev(1 if w == 0 else NX - 1)
        return rc(
            fsl(q, cs, NEAR[k]), fsl(q, 2 + 2 * w + cs, NEAR[k]),
            xs.at[k, q, w, cs], xv.at[k, q, w, cs], dev,
        )

    def send_x(q, cs, k):
        xw(q, cs, 0, k).start()
        xw(q, cs, 1, k).start()

    def step_a(k):
        @pl.loop(1, Q)
        def _(q):
            for cs in range(2):
                got(q, cs, k).wait_recv()
                send_x(q, cs, k)

    lanes_own = pl.ds(pl.multiple_of(c * FS, FS), FS)
    lanes_far = pl.ds(pl.multiple_of((6 + c) * FS, FS), FS)

    def near(k):
        part = NEAR[k]
        r0, r1 = part[0], part[0] + part[1]
        place(c, part)
        for a in range(2):
            RB[0, a, r0:r1, lanes_own] = gather(c, a, XB, part)
        send_x(0, c, k)
        place(1 - c, part)
        for a in range(2):
            GB[0, a, r0:r1] = gather(1 - c, a, XB, part)
        pc(k).start()

        @pl.loop(1, U)
        def _(u):
            q, j = pair(u)
            e = ((NY - q) % NY) * 2 + j
            place(e, part)
            for a in range(2):
                GB[u, a, r0:r1] = gather(e, a, XB, part)
            yc(u, k).start()

        got(0, 1 - c, k).wait_recv()
        send_x(0, 1 - c, k)

    def far(k):
        part = FAR[k]
        r0, r1 = part[0], part[0] + part[1]

        @pl.loop(1, U)
        def _(u):
            q, j = pair(u)
            e = ((NY - q) % NY) * 2 + j
            for a in range(2):
                GA[u, a, r0:r1] = gather(e, a, XA, part)
            ya(u, k).start()

        for a in range(2):
            GA[0, a, r0:r1] = gather(1 - c, a, XA, part)
        pa(k).start()
        for a in range(2):
            RB[0, a, r0:r1, lanes_far] = gather(c, a, XA, part)

    def ring_a(s):
        for a in range(2):
            for way in range(2):
                if s < half or a == way:
                    za(way, s, a).wait_recv()
                if s + 1 < half or (s + 1 == half and a == way):
                    za(way, s + 1, a).start()

    key(0)
    for d in range(NZ):
        T[d] = jnp.zeros((TOK, FS), F32)
        TF[d] = jnp.zeros((TOK, FS), F32)
    for s in range(1, half + 1):
        for way in range(2):
            if s < half or way == 0:
                zm(way, s).wait_recv()
                if s + 1 < half or (s + 1 == half and way == 0):
                    zm(way, s + 1).start()
        key(NZ - s)
        if s < half:
            key(s)
        for a in range(2):
            for way in range(2):
                if s < half or a == way:
                    zx(way, s, a).wait_recv()
                if s + 1 < half or (s + 1 == half and a == way):
                    zx(way, s + 1, a).start()
        if s == 1:
            near(0)
        elif s == 2:
            near(1)
        elif s == half - 1:
            for a in range(2):
                xa(a).wait_recv()
                for way in range(2):
                    za(way, 1, a).start()
            step_a(0)
        else:
            near(2)
    step_a(1)
    ring_a(1)
    ring_a(2)
    far(0)
    step_a(2)
    ring_a(3)
    ring_a(4)
    far(1)
    for m in range(3):
        for f in range(NF):
            wload(m, f).wait()
            wgive(m, f).wait_recv()

    nt = (((1,), (1,)), ((), ()))
    tn = (((0,), (0,)), ((), ()))

    def rm(q, w, cs):
        return rc(
            PB.at[q, 4 - 2 * w + cs], RM.at[q, w, cs], rs.at[q, w, cs], rv.at[q, w, cs],
            xdev(1 if w == 0 else NX - 1),
        )

    def ry(q, cs):
        dev = {"expert": ((y + q) % NY) * NZ + z, "ctx": x * 2 + cs}
        return rc(FB.at[q, cs], YB.at[q, c], rys.at[q, cs], ryv.at[q, c], dev)

    def fy(q, cs):
        dev = {"expert": ((y + q) % NY) * NZ + z, "ctx": x * 2 + cs}
        return rc(PB.at[q, 6 + cs], YF.at[q, c], fys.at[q, cs], fyv.at[q, c], dev)

    def fy_got(q, j):
        return rc(PB.at[q, 6], YF.at[q, j], fys.at[q, 0], fyv.at[q, j], partner)

    def ry_got(q, j):
        return rc(FB.at[q, 0], YB.at[q, j], rys.at[q, 0], ryv.at[q, j], partner)

    def step_d(q):
        for k in range(3):
            for cs in range(2):
                xw(q, cs, 0, k).wait_recv()
                xw(q, cs, 1, k).wait_recv()

        def own_far():
            got_a(q, c, 0).wait_recv()
            got_a(q, c, 1).wait_recv()

        got_a(q, 1 - c, 0).wait_recv()
        got_a(q, 1 - c, 1).wait_recv()
        pl.when(q > 0)(own_far)
        gate_up = WV[0:2].reshape(4 * FFL, D)
        pre = lax.dot_general(RB[q, 0], gate_up, nt, preferred_element_type=F32)
        hidden = lax.dot_general(RB[q, 1], WV[2], nt, preferred_element_type=F32)
        pre_gate, pre_up = pre[:, 0 : 2 * FFL], pre[:, 2 * FFL :]
        sg = jax.nn.sigmoid(pre_gate)
        act = pre_gate * sg
        prod = act * pre_up * hidden
        hi = prod.astype(BF)
        lo = (prod - hi.astype(F32)).astype(BF)
        ones = jnp.ones((8, 2 * FFL), BF)
        score = lax.dot_general(ones, hi, nt, preferred_element_type=F32)
        score = score + lax.dot_general(ones, lo, nt, preferred_element_type=F32)
        SC[q, :, 0:R] = score[0:1]

        @pl.when(q == Q - 1)
        def _():
            for k in range(1, NF):
                scx(k).start()

        gpg = (hidden * pre_up * sg * (1.0 + pre_gate * (1.0 - sg))).astype(BF)
        gpu = (hidden * act).astype(BF)
        both = jnp.concatenate([gpg, gpu], axis=1)
        for f in (6, 7, 4, 2, 5, 3, 0, 1):
            weights = WV[0:2, :, f * FS : (f + 1) * FS].reshape(4 * FFL, FS)
            PB[q, f] = jnp.dot(both, weights, preferred_element_type=F32).astype(BF)
            if f >= 6:
                cs = f - 6
                pl.when((q > 0) | (c != cs))(lambda: fy(q, cs).start())
            elif f >= 2:
                rm(q, 0 if f >= 4 else 1, f % 2).start()

    def step_g(q):
        def total(cs):
            for w in range(2):
                rm(q, w, cs).wait_recv()
            near = PB[q, cs].astype(F32) + RM[q, 0, cs].astype(F32)
            return (near + RM[q, 1, cs].astype(F32)).astype(BF)

        for cs in range(2):
            FB[q, cs] = total(cs)
            pl.when((q > 0) | (c != cs))(lambda: ry(q, cs).start())

    def combine_slab(q, rows_of, sums, d):
        e0 = ((NY - q) % NY) * 2
        for j in range(2):
            pick = PLB[e0 + j, :, d * TOK : (d + 1) * TOK].astype(F32)
            weight = WT[e0 + j, :, d * TOK : (d + 1) * TOK]
            pick = pick * jnp.broadcast_to(weight, (R, TOK))
            sums[d] += lax.dot_general(
                pick.astype(BF), rows_of[q, j], tn, preferred_element_type=F32
            )

    def combine(q, rows_of, sums):
        for d in range(NZ):
            combine_slab(q, rows_of, sums, d)

    def step_h(q):
        for j in range(2):
            pl.when((q > 0) | (c != j))(lambda: ry_got(q, j).wait_recv())

        @pl.when(q == 0)
        def _():
            YB[0, c] = FB[0, c]

        combine(q, YB, T)

    def step_hf(q):
        for j in range(2):
            pl.when((q > 0) | (c != j))(lambda: fy_got(q, j).wait_recv())

        @pl.when(q == 0)
        def _():
            YF[0, c] = PB[0, 6 + c]

        combine(q, YF, TF)

    def scx(k):
        return rc(SC, SCR.at[me_c], scs.at[k - 1], scv.at[k - 1], cdev(k))

    def scy(k):
        return rc(SCT, YSC.at[k - 1], sys_.at[k - 1], syv.at[k - 1], ydev(NY - k))

    def scz(k):
        return rc(SE.at[k], ZSC.at[NZ - k], szs.at[k - 1], szv.at[k - 1], zdev(k))

    hf = FS // 2

    class Ring:
        def __init__(self, sums, sent, came, ss, rs):
            self.sums, self.sent, self.came, self.ss, self.rs = sums, sent, came, ss, rs

        def copy(self, way, s, p):
            lanes = pl.ds(p * hf, hf)
            return rc(
                self.sent.at[way, s - 1, :, lanes], self.came.at[way, s - 1, :, lanes],
                self.ss.at[way, s - 1, p], self.rs.at[way, s - 1, p],
                zdev(1 if way == 0 else NZ - 1),
            )

        def hop(self, way, s, p):
            d = half - (s - 1) if way == 0 else half + (s - 1)
            lanes = slice(p * hf, (p + 1) * hf)
            value = self.sums[POS[d], :, lanes]
            if s > 2 or (s == 2 and p == way):
                self.copy(way, s - 1, p).wait_recv()
                value = value + self.came[way, s - 2, :, lanes].astype(F32)
            self.sent[way, s - 1, :, lanes] = value.astype(BF)
            self.copy(way, s, p).start()

        def begin(self):
            for way in range(2):
                self.hop(way, 1, way)
            for way in range(2):
                self.hop(way, 2, 1 - way)

        def step(self, s):
            for way in range(2):
                self.hop(way, s, way)
            if s > 2:
                for way in range(2):
                    self.hop(way, s, 1 - way)

        def result(self, p):
            lanes = slice(p * hf, (p + 1) * hf)
            value = self.sums[0, :, lanes]
            for way in range(2):
                self.copy(way, half, p).wait_recv()
                value = value + self.came[way, half - 1, :, lanes].astype(F32)
            return value

    near_ring = Ring(T, ZS, ZR, zrs, zrv)
    far_ring = Ring(TF, ZSF, ZRF, fzs, fzv)

    def swap():
        return rc(OS, OR, os_, ov, xdev(2))

    pl.loop(0, Q)(step_d)
    pl.loop(0, Q)(step_hf)
    far_ring.begin()
    step_g(0)
    step_g(1)
    far_ring.step(2)
    step_g(2)
    far_ring.step(3)
    step_g(3)
    pl.loop(0, Q - 1)(step_h)
    far_ring.step(4)

    for j in range(2):
        ry_got(Q - 1, j).wait_recv()
    for d in (4, 3, 5, 2, 6, 1, 7, 0):
        combine_slab(Q - 1, YB, T, POS[d])
        if d == half:
            for way in range(2):
                near_ring.hop(way, 1, way)
        elif d == half - 1:
            near_ring.hop(0, 2, 1)
        elif d == half + 1:
            near_ring.hop(1, 2, 0)
    SCR[me_c] = SC[...]
    for k in range(1, NF):
        scx(k).wait_recv()
    for j in range(2):
        total = SCR[j]
        for k in range(1, NX):
            total = total + SCR[2 * k + j]
        SCT[j] = total
    for k in range(1, NY):
        scy(k).start()
    near_ring.step(2)
    for p in range(2):
        OS[:, p * hf : (p + 1) * hf] = far_ring.result(p).astype(BF)
    swap().start()
    for dy in range(NY):
        if dy:
            scy(dy).wait_recv()
        for j in range(2):
            e = dy * 2 + j
            row = (NY - dy) % NY
            table = SCT[j, row, :, 0:R] if dy == 0 else YSC[dy - 1, j, row, :, 0:R]
            table = jnp.broadcast_to(table, (8, R))
            hi = table.astype(BF)
            lo = (table - hi.astype(F32)).astype(BF)
            spread = jnp.dot(hi, PLB[e], preferred_element_type=F32)
            spread = spread + jnp.dot(lo, PLB[e], preferred_element_type=F32)
            for d in range(NZ):
                SE[d, e : e + 1, :] = spread[0:1, POS[d] * TOK : (POS[d] + 1) * TOK]
    for k in range(1, NZ):
        scz(k).start()
    near_ring.step(3)
    near_ring.step(4)

    gates = jnp.zeros((TOP, TOK), F32)
    ids = MB[0, 0:TOP, :]
    for d in range(NZ):
        if d:
            scz(NZ - d).wait_recv()
        piece = SE[0] if d == 0 else ZSC[d]
        for i in range(8):
            who = (2 * (((y + i // 2) % NY) * NZ + (z + d) % NZ) + i % 2).astype(F32)
            gates = gates + jnp.where(
                ids == who, jnp.broadcast_to(piece[i : i + 1, :], (TOP, TOK)), 0.0
            )
    gg[...] = gates.astype(BF)

    swap().wait_recv()
    for p in range(2):
        lanes = slice(p * hf, (p + 1) * hf)
        out[:, lanes] = (near_ring.result(p) + OR[:, lanes].astype(F32)).astype(BF)

    for m in range(3):
        for f in range(NF):
            wgive(m, f).wait_send()
    for a in range(2):
        xa(a).wait_send()
    for s in range(1, half + 1):
        for way in range(2):
            if s < half or way == 0:
                zm(way, s).wait_send()
            for a in range(2):
                if s < half or a == way:
                    zx(way, s, a).wait_send()
                    za(way, s, a).wait_send()
                if s > 1 or a == way:
                    near_ring.copy(way, s, a).wait_send()
                    far_ring.copy(way, s, a).wait_send()

    @pl.loop(0, Q)
    def _(q):
        for w in range(2):
            for cs in range(2):
                for k in range(3):
                    xw(q, cs, w, k).wait_send()
                rm(q, w, cs).wait_send()
        for cs in range(2):
            pl.when((q > 0) | (c != cs))(lambda: ry(q, cs).wait_send())
            pl.when((q > 0) | (c != cs))(lambda: fy(q, cs).wait_send())

    swap().wait_send()
    for k in range(3):
        pc(k).wait_send()
    for k in range(2):
        pa(k).wait_send()

    @pl.loop(1, U)
    def _(u):
        for k in range(3):
            yc(u, k).wait_send()
        for k in range(2):
            ya(u, k).wait_send()

    for k in range(1, NF):
        scx(k).wait_send()
    for k in range(1, NY):
        scy(k).wait_send()
    for k in range(1, NZ):
        scz(k).wait_send()


def body(tokens, grad_out, expert_ids, gate_probs, gate_weight, up_weight, down_weight):
    V, S = pltpu.VMEM, pltpu.SemaphoreType.DMA
    scratch = [
        V((NZ, 2, TOK, FS), BF), V((NZ, 2, TOK, FS), BF), V((NZ, 2 * TOP, TOK), F32),
        V((8, 1, NZ * TOK), F32), V((8, 1, NZ * TOK), F32), V((8, R, NZ * TOK), BF),
        V((U, 2, R, FS), BF), V((U, 2, R, FS), BF), V((Q, 2, R, D), BF), V((3, 2 * FFL, D), BF),
        V((Q, NF, R, FS), BF), V((Q, 2, 2, R, FS), BF),
        V((Q, 2, R, FS), BF), V((Q, 2, R, FS), BF), V((Q, 2, R, FS), BF),
        V((NZ, TOK, FS), F32), V((NZ, TOK, FS), F32),
        V((2, NZ // 2, TOK, FS), BF), V((2, NZ // 2, TOK, FS), BF),
        V((2, NZ // 2, TOK, FS), BF), V((2, NZ // 2, TOK, FS), BF),
        V((TOK, FS), BF), V((TOK, FS), BF),
        V((Q, 1, 256), F32), V((NF, Q, 1, 256), F32), V((2, Q, 1, 256), F32),
        V((NY - 1, 2, Q, 1, 256), F32), V((NZ, 8, TOK), F32), V((NZ, 8, TOK), F32),
        S((2,)), S((3, NF)), S((3, NF)), S((3, NF)),
        S((2, 4, 2)), S((2, 4, 2)), S((2, 4, 2)), S((2, 4, 2)), S((2,)), S((2,)),
        S((2, 4)), S((2, 4)), S((3, U)), S((3, Q, 2)), S((2, U)), S((2, Q, 2)),
        S((3, Q, 2, 2)), S((3, Q, 2, 2)),
        S((Q, 2)), S((Q, 2)), S((Q, 2, 2)), S((Q, 2, 2)), S((Q, 2)), S((Q, 2)),
        S((2, 4, 2)), S((2, 4, 2)), S((2, 4, 2)), S((2, 4, 2)), S(()), S(()),
        S((NF - 1,)), S((NF - 1,)), S((NY - 1,)), S((NY - 1,)), S((NZ - 1,)), S((NZ - 1,)),
    ]
    anyspec = pl.BlockSpec(memory_space=pl.ANY)
    vmem = pl.BlockSpec(memory_space=pltpu.VMEM)
    out, gates = pl.pallas_call(
        kernel,
        out_shape=(
            jax.ShapeDtypeStruct((TOK, FS), BF),
            jax.ShapeDtypeStruct((TOP, TOK), BF),
        ),
        in_specs=[anyspec] * 2 + [vmem] * 2 + [anyspec] * 3,
        out_specs=(vmem, vmem),
        scratch_shapes=scratch,
        compiler_params=pltpu.CompilerParams(
            collective_id=0, has_side_effects=True, vmem_limit_bytes=60 * 1024 * 1024
        ),
        name="expert_grad",
    )(tokens, grad_out, expert_ids.T, gate_probs.T, gate_weight, up_weight, down_weight)
    return out, gates.T


def solution(mesh):
    in_specs = (
        P("expert", "ctx"),
        P("expert", "ctx"),
        P("expert", None),
        P("expert", None),
        P("expert", "ctx", None),
        P("expert", "ctx", None),
        P("expert", "ctx", None),
    )
    out_specs = (P("expert", "ctx"), P("expert", None))
    return jax.shard_map(body, mesh=mesh, in_specs=in_specs, out_specs=out_specs, check_vma=False)
```
